32 devices in a mesh: dp: 8 (over z, core), seq: 4 (over y, x).
Axes of the slice: x: 2, y: 2, z: 4, core: 2. Of those that a mesh axis runs over, the one named last changes fastest.
Arguments:
- tokens_in: bfloat16 [16384, 1024], P(('dp', 'seq')), may hold values from -6 to 6
- norm_attn: bfloat16 [1024], P('dp'), may hold values from 0.5 to 1.5
- w_query: bfloat16 [1024, 1024], P('dp'), may hold values from -0.1875 to 0.1875
- key_value_weight: bfloat16 [1024, 1024], P('dp'), may hold values from -0.1875 to 0.1875
- gain_query: bfloat16 [64], P('dp'), may hold values from 1 to 2
- gain_key: bfloat16 [64], P('dp'), may hold values from 1 to 2
- w_out: bfloat16 [1024, 1024], P('dp'), may hold values from -0.75 to 0.75
- norm_ffn: bfloat16 [1024], P('dp'), may hold values from 0.5 to 1.5
- w_gate: bfloat16 [1024, 4608], P(None, 'dp'), may hold values from -0.1875 to 0.1875
- w_up: bfloat16 [1024, 4608], P(None, 'dp'), may hold values from -0.1875 to 0.1875
- w_down: bfloat16 [4608, 1024], P('dp'), may hold values from -0.09375 to 0.09375
- cotangent: bfloat16 [16384, 1024], P(('dp', 'seq')), may hold values from -6 to 6
- segments: int32 [8, 2048], P('dp'), may hold values from 0 to 3, never falling along the last dimension, each value on 1 to 1024 neighbouring positions
- blocks: int32 [8, 16], P('dp'), may hold values from 0 to 15, each once within a row
Outputs:
- output: bfloat16 [16384, 1024], P(('dp', 'seq'))
- grad_tokens: float32 [16384, 1024], P(('dp', 'seq'))
- grad_norm_attn: float32 [1024], P('dp')
- grad_w_query: float32 [1024, 1024], P('dp')
- grad_w_keyval: float32 [1024, 1024], P('dp')
- grad_gain_query: float32 [64], P('dp')
- grad_gain_key: float32 [64], P('dp')
- grad_w_out: float32 [1024, 1024], P('dp')
- grad_norm_ffn: float32 [1024], P('dp')
- grad_w_gate: float32 [1024, 4608], P(None, 'dp')
- grad_w_up: float32 [1024, 4608], P(None, 'dp')
- grad_w_down: float32 [4608, 1024], P('dp')
The draws below stay inside these ranges and needn't reach their ends.
Inputs may be any that keep to these rules, and one draw needn't show every extreme that they name: `segments`: in each row the document numbers never fall, all 4 documents occur, each covers 1 to 1024 places and the longest exactly 1024. `blocks`: each row holds every block number once.
All inputs are finite; a program needn't handle non-finite values.
Results may differ from the reference program's by a relative error of at most 0.025.
Values may be sent and summed in bfloat16 or wider, within the bound.
A program may use at most 192 MiB of HBM per device.

```python
import math
from functools import partial
import jax
import jax.numpy as jnp
import numpy as np
from jax import lax

MODEL_WIDTH = 1024
QUERY_HEADS = 16
KEY_VALUE_HEADS = 8
HEAD_SIZE = 64
FF = 4608
BLOCK = 128
QUERY_ROWS = 512
GROUP_TOKENS = 2048
GROUPS = 8
TOKENS = 16384
BLOCKS = 16
DOC_MOST = 1024
DOCS = 4


def steps_of(key, extent, cuts, smallest, top_value):
    def one(position, shards_of):
        heights = jax.random.uniform(jax.random.fold_in(jax.random.fold_in(key, 6), position), (shards_of,), jnp.float32, smallest / len(cuts), top_value / len(cuts))
        return jnp.repeat(jnp.exp(heights), extent[position] // shards_of).reshape((-1,) + (1,) * (len(extent) - position - 1))

    factor_of = one(*cuts[0])
    for cut in cuts[1:]:
        factor_of = factor_of * one(*cut)
    return factor_of


def split_up(number_of, total, reach, skew):
    weights = [(1 << 20) // math.isqrt(rank ** skew) + 1 for rank in range(2, number_of + 1)]
    spare, holding = total - reach - (number_of - 1), [1] * (number_of - 1)
    while spare > 0:
        free = [i for i in range(number_of - 1) if holding[i] < reach]
        whole, remaining = sum([weights[i] for i in free]), spare
        for i in free:
            addition = min(reach - holding[i], max(1, remaining * weights[i] // whole), spare)
            holding[i] = holding[i] + addition
            spare = spare - addition
    return np.array([reach] + holding)


def uneven(own_key, number_of, total, reach, slope):
    if number_of == 2:
        one = jax.random.randint(own_key, (), max(1, total - reach), min(reach, total - 1) + 1)
        return jnp.stack([one, total - one])
    sizes = jnp.asarray(split_up(number_of, total, reach, slope), jnp.int32)
    pairs = (number_of - 1) // 2
    donor, taker = sizes[1:1 + 2 * pairs:2], sizes[2:2 + 2 * pairs:2]
    margin = jnp.minimum(donor - 1, reach - taker)
    passed = jax.random.randint(jax.random.fold_in(own_key, 1), (pairs,), 0, 1 << 20) % (margin + 1)
    sizes = sizes.at[1:1 + 2 * pairs:2].set(donor - passed).at[2:2 + 2 * pairs:2].set(taker + passed)
    return sizes[jax.random.permutation(jax.random.fold_in(own_key, 2), number_of)]


def scatter_about(rng, extent, width, reach, shards=(), held_as=jnp.bfloat16):
    drawn = jax.random.normal(rng, extent, jnp.float32) * width
    if len(shards) > 0:
        drawn = steps_of(rng, extent, shards, -0.22, 0.18) * drawn
    return jnp.clip(drawn, min=-reach, max=reach).astype(held_as)


def setup_inputs(seed: int = 0) -> dict:
    keys = jax.random.split(jax.random.key(seed), 15)
    tokens_in = scatter_about(keys[0], (TOKENS, MODEL_WIDTH), 1.0, 6.0, ((0, 32),))
    norm_attn = jnp.clip(1.0 + 0.1 * jax.random.normal(keys[1], (MODEL_WIDTH,), jnp.float32), 0.5, 1.5).astype(jnp.bfloat16)
    w_query = scatter_about(keys[2], (MODEL_WIDTH, QUERY_HEADS * HEAD_SIZE), MODEL_WIDTH ** -0.5, 0.1875, ((0, 8),))
    key_value_weight = scatter_about(keys[3], (MODEL_WIDTH, 2 * KEY_VALUE_HEADS * HEAD_SIZE), MODEL_WIDTH ** -0.5, 0.1875, ((0, 8),))
    gain_query = jnp.clip(1.0 + 1.0 * jax.random.uniform(keys[4], (HEAD_SIZE,), jnp.float32) ** steps_of(keys[4], (HEAD_SIZE,), ((0, 8),), -0.2, 0.2), 1.0, 2.0).astype(jnp.bfloat16)
    gain_key = jnp.clip(1.0 + 1.0 * jax.random.uniform(keys[5], (HEAD_SIZE,), jnp.float32) ** steps_of(keys[5], (HEAD_SIZE,), ((0, 8),), -0.2, 0.2), 1.0, 2.0).astype(jnp.bfloat16)
    w_out = scatter_about(keys[6], (QUERY_HEADS * HEAD_SIZE, MODEL_WIDTH), HEAD_SIZE ** -0.5, 0.75, ((0, 8),))
    norm_ffn = jnp.clip(1.0 + 0.1 * jax.random.normal(keys[7], (MODEL_WIDTH,), jnp.float32), 0.5, 1.5).astype(jnp.bfloat16)
    w_gate = scatter_about(keys[8], (MODEL_WIDTH, FF), MODEL_WIDTH ** -0.5, 0.1875, ((1, 8),))
    w_up = scatter_about(keys[9], (MODEL_WIDTH, FF), MODEL_WIDTH ** -0.5, 0.1875, ((1, 8),))
    w_down = scatter_about(keys[10], (FF, MODEL_WIDTH), FF ** -0.5, 0.09375, ((0, 8),))
    cotangent = scatter_about(keys[11], (TOKENS, MODEL_WIDTH), 1.0, 6.0, ((0, 32),))
    segments = jax.vmap(lambda own: jnp.searchsorted(jnp.cumsum(uneven(own, DOCS, GROUP_TOKENS, DOC_MOST, 2)), jnp.arange(GROUP_TOKENS), side="right"))(jax.random.split(keys[12], GROUPS)).reshape((GROUPS, GROUP_TOKENS)).astype(jnp.int32)
    blocks = jax.vmap(lambda own: jax.random.permutation(own, BLOCKS))(jax.random.split(keys[13], GROUPS)).reshape((GROUPS, BLOCKS)).astype(jnp.int32)
    return dict(tokens_in=tokens_in, norm_attn=norm_attn, w_query=w_query, key_value_weight=key_value_weight, gain_query=gain_query, gain_key=gain_key, w_out=w_out, norm_ffn=norm_ffn, w_gate=w_gate, w_up=w_up, w_down=w_down, cotangent=cotangent, segments=segments, blocks=blocks)


EPS = 1e-05
THETA = 1000000.0
MASKED = -1e+30
HIGH = lax.Precision.HIGHEST

@jax.custom_vjp
def low(v):
    return lax.optimization_barrier(v.astype(jnp.bfloat16)).astype(jnp.float32)

@jax.custom_vjp
def reduced_backward(v):
    return v

def low_keep(v):
    return (low(v), None)

def low_pass(kept, grad):
    return (grad,)

def back_keep(v):
    return (v, None)

def back_low(kept, grad):
    return (low(grad),)
low.defvjp(low_keep, low_pass)
reduced_backward.defvjp(back_keep, back_low)

def matrix_product(left_op, right_op):
    return jnp.dot(left_op, right_op, precision=HIGH, preferred_element_type=jnp.float32)

def normed(tensor, gain_vec):
    factor = lax.rsqrt(lax.optimization_barrier(jnp.mean(tensor * tensor, axis=-1, keepdims=True)) + EPS)
    return tensor * factor * gain_vec

def rotate(tensor, angle_cos, angle_sin):
    half_dim = tensor.shape[-1] // 2
    front_half = tensor[..., :half_dim]
    back_half = tensor[..., half_dim:]
    return jnp.concatenate([front_half * angle_cos - back_half * angle_sin, back_half * angle_cos + front_half * angle_sin], axis=-1)

def angles(offsets, head_dim):
    half_dim = head_dim // 2
    frequency = jnp.exp(jnp.arange(half_dim, dtype=jnp.float32) * (-2.0 * math.log(THETA) / head_dim))
    turned = offsets.astype(jnp.float32)[:, None] * frequency[None, :]
    return (jnp.cos(turned)[:, None, :], jnp.sin(turned)[:, None, :])

def layout(segment_row, order_row, block_len):
    length_all = segment_row.shape[0]
    places = jnp.arange(length_all, dtype=jnp.int32)
    seg_start = jnp.concatenate([jnp.ones((1,), dtype=bool), segment_row[1:] != segment_row[:-1]])
    starts = lax.cummax(jnp.where(seg_start, places, 0), axis=0)
    offsets = places - starts
    placed_tokens = (order_row[:, None] * block_len + jnp.arange(block_len, dtype=jnp.int32)[None, :]).reshape(length_all)
    return (placed_tokens, segment_row[placed_tokens], offsets[placed_tokens])

def attend_within_group(query_matrix, key_rows, value_rows, placed_tokens, documents_for_rows):
    group_len = query_matrix.shape[0]
    repeat_factor = query_matrix.shape[1] // key_rows.shape[1]
    keys_wide = jnp.repeat(key_rows, repeat_factor, axis=1)
    values_wide = jnp.repeat(value_rows, repeat_factor, axis=1)
    factor = query_matrix.shape[2] ** (-0.5)

    def block_out(group_members):
        query_rows, placed_rows, docs_rows = group_members
        raw_scores = reduced_backward(jnp.einsum('rhd,jhd->hrj', query_rows, keys_wide, precision=HIGH) * factor)
        allowed = (docs_rows[:, None] == documents_for_rows[None, :]) & (placed_tokens[None, :] <= placed_rows[:, None])
        masked = jnp.where(allowed[None], raw_scores, MASKED)
        row_top = lax.optimization_barrier(jnp.max(masked, axis=-1, keepdims=True))
        exponent = jnp.exp(masked - row_top)
        weights = low(exponent / lax.optimization_barrier(jnp.sum(exponent, axis=-1, keepdims=True)))
        return jnp.einsum('hrj,jhd->rhd', weights, values_wide, precision=HIGH)
    count_blocks = group_len // QUERY_ROWS
    result = lax.map(jax.checkpoint(block_out), (query_matrix.reshape(count_blocks, QUERY_ROWS, query_matrix.shape[1], query_matrix.shape[2]), placed_tokens.reshape(count_blocks, QUERY_ROWS), documents_for_rows.reshape(count_blocks, QUERY_ROWS)))
    return result.reshape(query_matrix.shape)

def reference(tokens_in, norm_attn, w_query, key_value_weight, gain_query, gain_key, w_out, norm_ffn, w_gate, w_up, w_down, cotangent, segments, blocks):
    placed_tokens, documents_for_rows, offsets = jax.vmap(partial(layout, block_len=BLOCK))(segments, blocks)
    count_of_rows = tokens_in.shape[0]
    count_of_groups = placed_tokens.shape[0]
    angle_cos, angle_sin = angles(offsets.reshape(count_of_rows), HEAD_SIZE)

    def forward(hidden, gain_attn, query_w, key_value_matrix, query_gain, key_gain, out_w, gain_ffn, gate_w, up_w, down_w):
        normalized_input = low(normed(hidden, gain_attn))
        query_raw = reduced_backward(matrix_product(normalized_input, query_w)).reshape(count_of_rows, QUERY_HEADS, HEAD_SIZE)
        key_value_unrotated = reduced_backward(matrix_product(normalized_input, key_value_matrix)).reshape(count_of_rows, KEY_VALUE_HEADS, 2, HEAD_SIZE)
        query_matrix = low(reduced_backward(rotate(normed(query_raw, query_gain), angle_cos, angle_sin)))
        key_rows = low(reduced_backward(rotate(normed(key_value_unrotated[:, :, 0], key_gain), angle_cos, angle_sin)))
        value_rows = low(reduced_backward(key_value_unrotated[:, :, 1]))
        attention_mixed = lax.map(lambda group_members: attend_within_group(*group_members), (query_matrix.reshape(count_of_groups, GROUP_TOKENS, QUERY_HEADS, HEAD_SIZE), key_rows.reshape(count_of_groups, GROUP_TOKENS, KEY_VALUE_HEADS, HEAD_SIZE), value_rows.reshape(count_of_groups, GROUP_TOKENS, KEY_VALUE_HEADS, HEAD_SIZE), placed_tokens, documents_for_rows))
        attended = low(reduced_backward(attention_mixed.reshape(count_of_rows, QUERY_HEADS * HEAD_SIZE)))
        middle = hidden + reduced_backward(matrix_product(attended, out_w))
        ffn_in = low(normed(middle, gain_ffn))
        gate_pre = reduced_backward(matrix_product(ffn_in, gate_w))
        up_pre = reduced_backward(matrix_product(ffn_in, up_w))
        activated = low(jax.nn.silu(gate_pre) * up_pre)
        return middle + reduced_backward(matrix_product(activated, down_w))
    params = (tokens_in.astype(jnp.float32), norm_attn.astype(jnp.float32), w_query.astype(jnp.float32), key_value_weight.astype(jnp.float32), gain_query.astype(jnp.float32), gain_key.astype(jnp.float32), w_out.astype(jnp.float32), norm_ffn.astype(jnp.float32), w_gate.astype(jnp.float32), w_up.astype(jnp.float32), w_down.astype(jnp.float32))
    output, pullback = jax.vjp(forward, *params)
    gradients = pullback(cotangent.astype(jnp.float32))
    return (output.astype(jnp.bfloat16), gradients[0], gradients[1], gradients[2], gradients[3], gradients[4], gradients[5], gradients[6], gradients[7], gradients[8], gradients[9], gradients[10])
```

```python
import functools
import math

import jax
import jax.numpy as jnp
from jax import lax
from jax.experimental import pallas as pl
from jax.experimental.pallas import tpu as pltpu
from jax.sharding import PartitionSpec as P

KEY_VALUE_HEADS = 8
HEAD = 64
PAIR = 2 * HEAD
BLOCK = 128
SPAN = 256
EPS = 1e-05
THETA = 1000000.0
MOST_DOCS = 8
F32 = jnp.float32
BF16 = jnp.bfloat16
VMEM = pltpu.VMEM
LIMIT = 66000000


def nn(a, b):
    return lax.dot_general(a, b, (((1,), (0,)), ((), ())), preferred_element_type=F32)


def nt(a, b):
    return lax.dot_general(a, b, (((1,), (1,)), ((), ())), preferred_element_type=F32)


def tn(a, b):
    return lax.dot_general(a, b, (((0,), (0,)), ((), ())), preferred_element_type=F32)


def split_dot(a, b):
    high = a.astype(BF16)
    low = (a - high.astype(F32)).astype(BF16)
    return nn(high, b) + nn(low, b)


def lanes(shape):
    return lax.broadcasted_iota(jnp.int32, shape, len(shape) - 1)


def head_mean(wide):
    row = lax.broadcasted_iota(jnp.int32, (wide, wide), 0) // HEAD
    col = lax.broadcasted_iota(jnp.int32, (wide, wide), 1) // HEAD
    return jnp.where(row == col, 1.0 / HEAD, 0.0).astype(BF16)


def partner(u):
    wide, half = u.shape[-1], HEAD // 2
    front = lanes(u.shape) % HEAD < half
    return jnp.where(front, pltpu.roll(u, wide - half, 1), pltpu.roll(u, half, 1))


def swap_heads(u):
    return pltpu.roll(u, HEAD, 1)


def tile_lanes(u, times):
    return u if times == 1 else jnp.concatenate([u] * times, axis=1)


def attend_kernel(groups, inv, first, q_raw, kv_raw, cos, sin, starts, gain_q, gain_kv,
                  o_ref, qs, kvs, linv, ov):
    blocks = inv.shape[0]
    wide = q_raw.shape[1]
    mean = head_mean(wide)
    low_half = lanes((BLOCK, PAIR)) < HEAD
    is_key = lanes((BLOCK, wide)) % PAIR < HEAD

    def prepare(p, _):
        rows = pl.ds(pl.multiple_of(inv[p] * BLOCK, BLOCK), BLOCK)
        place = pl.ds(pl.multiple_of(p * BLOCK, BLOCK), BLOCK)
        c = tile_lanes(cos[place, :], groups)
        s = tile_lanes(sin[place, :], groups)

        def turned(raw, gain):
            u = raw * lax.rsqrt(split_dot(raw * raw, mean) + EPS) * gain
            return u * c + partner(u) * s

        q = turned(q_raw[rows, :], gain_q[...]) * (HEAD ** -0.5)
        kv = kv_raw[rows, :]
        kv = jnp.where(is_key, turned(kv, gain_kv[...]), kv)
        for g in range(groups):
            pair = q[:, g * PAIR:(g + 1) * PAIR]
            qs[g, pl.ds(pl.multiple_of(p * SPAN, SPAN), BLOCK), :] = jnp.where(low_half, pair, 0.0).astype(BF16)
            qs[g, pl.ds(pl.multiple_of(p * SPAN + BLOCK, BLOCK), BLOCK), :] = jnp.where(
                low_half, swap_heads(pair), 0.0).astype(BF16)
            one = kv[:, g * PAIR:(g + 1) * PAIR]
            kvs[g, place, :] = one.astype(BF16)
            ov[g, place, :] = jnp.where(low_half, 1.0, one).astype(BF16)
        return 0

    lax.fori_loop(0, blocks, prepare, 0)
    for g in range(groups):
        kvs[g, blocks * BLOCK:, :] = jnp.zeros((BLOCK, PAIR), BF16)
        ov[g, blocks * BLOCK:, :] = jnp.zeros((BLOCK, PAIR), BF16)

    def one_block(p, _):
        base = p * BLOCK
        row = base + lax.broadcasted_iota(jnp.int32, (BLOCK, SPAN), 0)
        start = tile_lanes(starts[pl.ds(pl.multiple_of(base, BLOCK), BLOCK), :], SPAN // BLOCK)
        begin = first[p]

        def step(i, totals):
            at = pl.multiple_of((begin + 2 * i) * BLOCK, BLOCK)
            col = at + lanes((BLOCK, SPAN))
            allowed = (col >= start) & (col <= row)
            keys = pl.ds(at, SPAN)
            result = []
            for g in range(groups):
                score = nt(qs[g, pl.ds(pl.multiple_of(p * SPAN, SPAN), SPAN), :], kvs[g, keys, :])
                e = jnp.exp(score)
                e = jnp.concatenate([jnp.where(allowed, e[:BLOCK], 0.0), jnp.where(allowed, e[BLOCK:], 0.0)], axis=0)
                result.append(totals[g] + nn(e.astype(BF16), ov[g, keys, :]))
            return tuple(result)

        totals = lax.fori_loop(
            0, (p - begin) // 2 + 1, step, tuple(jnp.zeros((SPAN, PAIR), F32) for _ in range(groups)))
        rows = pl.ds(pl.multiple_of(inv[p] * BLOCK, BLOCK), BLOCK)
        for g in range(groups):
            total = totals[g]
            linv[g, p, :, :] = 1.0 / jnp.transpose(total)[0:8, :]
            one, two = total[:BLOCK], total[BLOCK:]
            o = jnp.where(low_half, swap_heads(one) / one, two / swap_heads(two))
            o_ref[rows, g * PAIR:(g + 1) * PAIR] = o.astype(BF16)
        return 0

    lax.fori_loop(0, blocks, one_block, 0)


def attend(inv, first, q_raw, kv_raw, cos, sin, starts, gain_q, gain_kv):
    rows, wide = q_raw.shape
    groups = wide // PAIR
    blocks = rows // BLOCK
    whole = pl.BlockSpec(memory_space=VMEM)
    return pl.pallas_call(
        functools.partial(attend_kernel, groups),
        out_shape=(
            jax.ShapeDtypeStruct((rows, wide), BF16),
            jax.ShapeDtypeStruct((groups, rows * 2, PAIR), BF16),
            jax.ShapeDtypeStruct((groups, rows + BLOCK, PAIR), BF16),
            jax.ShapeDtypeStruct((groups, blocks, 8, SPAN), F32),
        ),
        in_specs=[pl.BlockSpec(memory_space=pltpu.SMEM)] * 2 + [whole] * 7,
        out_specs=(whole,) * 4,
        scratch_shapes=[VMEM((groups, rows + BLOCK, PAIR), BF16)],
        compiler_params=pltpu.CompilerParams(vmem_limit_bytes=LIMIT),
        name="attend",
    )(inv, first, q_raw, kv_raw, cos, sin, starts, gain_q, gain_kv)


def attend_back_kernel(groups, inv, first, q_raw, kv_raw, cos, sin, starts, gain_q, gain_kv, o_ref, do_ref,
                       qs, kvs, linv, dq_ref, dkv_ref, gains_ref, kt, dkv, dq):
    blocks = inv.shape[0]
    wide = q_raw.shape[1]
    mean = head_mean(wide)
    low_half = lanes((BLOCK, PAIR)) < HEAD
    is_key = lanes((BLOCK, wide)) % PAIR < HEAD
    pick = (lax.broadcasted_iota(jnp.int32, (16, PAIR), 1) // HEAD
            == lax.broadcasted_iota(jnp.int32, (16, PAIR), 0) // 8).astype(BF16)

    dkv[...] = jnp.zeros_like(dkv)

    def turn_keys(p, _):
        place = pl.ds(pl.multiple_of(p * BLOCK, BLOCK), BLOCK)
        for g in range(groups):
            kt[g, :, place] = jnp.transpose(kvs[g, place, :].astype(F32))[:HEAD].astype(BF16)
        return 0

    lax.fori_loop(0, blocks, turn_keys, 0)
    for g in range(groups):
        kt[g, :, blocks * BLOCK:] = jnp.zeros((HEAD, BLOCK), BF16)

    def one_block(p, _):
        base = p * BLOCK
        rows = pl.ds(pl.multiple_of(inv[p] * BLOCK, BLOCK), BLOCK)
        queries = pl.ds(pl.multiple_of(p * SPAN, SPAN), SPAN)
        place_q = base + lanes((SPAN, SPAN)) % BLOCK
        start = jnp.broadcast_to(tile_lanes(starts[p, 0:1, :], 2), (SPAN, SPAN))
        begin = first[p]
        grads, dots = [], []
        for g in range(groups):
            pair = do_ref[rows, g * PAIR:(g + 1) * PAIR].astype(F32)
            grads.append(jnp.concatenate(
                [jnp.where(low_half, 0.0, swap_heads(pair)), jnp.where(low_half, 0.0, pair)], axis=0).astype(BF16))
            prod = pair * o_ref[rows, g * PAIR:(g + 1) * PAIR].astype(F32)
            high = prod.astype(BF16)
            low = (prod - high.astype(F32)).astype(BF16)
            d = nt(pick, high) + nt(pick, low)
            dots.append(jnp.concatenate([d[0:1], d[8:9]], axis=1))

        def step(i, totals):
            at = pl.multiple_of((begin + 2 * i) * BLOCK, BLOCK)
            keys = pl.ds(at, SPAN)
            place_k = at + lax.broadcasted_iota(jnp.int32, (SPAN, SPAN), 0)
            allowed = (place_k >= start) & (place_k <= place_q)
            result = []
            for g in range(groups):
                q = qs[g, queries, :]
                kv = kvs[g, keys, :]
                p_t = jnp.where(allowed, jnp.exp(nt(kv, q)) * linv[g, p, 0:1, :], 0.0)
                ds_t = (p_t * (nt(kv, grads[g]) - dots[g])).astype(BF16)
                dkv[g, keys, :] += nn(ds_t, q) + nn(p_t.astype(BF16), grads[g])
                result.append(totals[g] + nn(kt[g, :, keys], ds_t))
            return tuple(result)

        totals = lax.fori_loop(
            0, (p - begin) // 2 + 1, step, tuple(jnp.zeros((HEAD, SPAN), F32) for _ in range(groups)))
        for g in range(groups):
            total = totals[g]
            stacked = jnp.concatenate([total[:, :BLOCK], total[:, BLOCK:]], axis=0)
            dq[pl.ds(pl.multiple_of(base, BLOCK), BLOCK), g * PAIR:(g + 1) * PAIR] = (
                jnp.transpose(stacked) * (HEAD ** -0.5))
        return 0

    lax.fori_loop(0, blocks, one_block, 0)

    def finish(p, sums):
        rows = pl.ds(pl.multiple_of(inv[p] * BLOCK, BLOCK), BLOCK)
        place = pl.ds(pl.multiple_of(p * BLOCK, BLOCK), BLOCK)
        c = tile_lanes(cos[place, :], groups)
        s = tile_lanes(sin[place, :], groups)

        def back(raw, gain, grad):
            u = grad.astype(BF16).astype(F32)
            u = u * c - partner(u) * s
            factor = lax.rsqrt(split_dot(raw * raw, mean) + EPS)
            n = raw * factor
            term = u * n
            return factor * (u * gain - n * split_dot(term * gain, mean)), term

        dq_raw, q_term = back(q_raw[rows, :], gain_q[...], dq[place, :])
        dq_ref[rows, :] = dq_raw.astype(BF16)
        grad = jnp.concatenate([dkv[g, place, :] for g in range(groups)], axis=1)
        dk_raw, k_term = back(kv_raw[rows, :], gain_kv[...], grad)
        dkv_ref[rows, :] = jnp.where(is_key, dk_raw, grad).astype(BF16)

        def folded(term):
            return jnp.sum(term.reshape(BLOCK // 8, 8, wide), axis=0)

        return sums[0] + folded(q_term), sums[1] + folded(k_term)

    zero = jnp.zeros((8, wide), F32)
    sums = lax.fori_loop(0, blocks, finish, (zero, zero))
    gains_ref[0:8, :] = sums[0]
    gains_ref[8:16, :] = sums[1]


def attend_back(inv, first, q_raw, kv_raw, cos, sin, starts, gain_q, gain_kv, o, do, qs, kvs, linv):
    rows, wide = q_raw.shape
    groups = wide // PAIR
    whole = pl.BlockSpec(memory_space=VMEM)
    return pl.pallas_call(
        functools.partial(attend_back_kernel, groups),
        out_shape=(
            jax.ShapeDtypeStruct((rows, wide), BF16),
            jax.ShapeDtypeStruct((rows, wide), BF16),
            jax.ShapeDtypeStruct((16, wide), F32),
        ),
        in_specs=[pl.BlockSpec(memory_space=pltpu.SMEM)] * 2 + [whole] * 12,
        out_specs=(whole,) * 3,
        scratch_shapes=[
            VMEM((groups, HEAD, rows + BLOCK), BF16),
            VMEM((groups, rows + BLOCK, PAIR), F32),
            VMEM((rows, wide), F32),
        ],
        compiler_params=pltpu.CompilerParams(vmem_limit_bytes=LIMIT),
        name="attend_back",
    )(inv, first, q_raw, kv_raw, cos, sin, starts, gain_q, gain_kv, o, do, qs, kvs, linv)


def ffn_kernel(tile, x_ref, o_ref, gy_ref, w_out, gain, w_hbm, y_ref, db_ref, grad_hbm,
               w, total, b_s, y_s, db_s, out_s, sems):
    step = pl.program_id(0)
    pieces, _, part, width = w_hbm.shape
    hidden = pieces * part

    def copies(source, target):
        for k in range(3):
            for d in range(pieces):
                yield source, target, k, d

    def load(k, d):
        return pltpu.make_async_copy(w_hbm.at[d, k], w.at[k, pl.ds(d * part, part), :], sems.at[k, d])

    def store(k, d):
        return pltpu.make_async_copy(out_s.at[k, pl.ds(d * part, part), :], grad_hbm.at[d, k], sems.at[k, d])

    @pl.when(step == 0)
    def _():
        for k in range(3):
            for d in range(pieces):
                load(k, d).start()
        total[...] = jnp.zeros_like(total)
        for k in range(3):
            for d in range(pieces):
                load(k, d).wait()

    x1 = x_ref[...].astype(F32) + nn(o_ref[...], w_out[...])
    scale = lax.rsqrt(jnp.mean(x1 * x1, axis=-1, keepdims=True) + EPS)
    b_s[...] = (x1 * scale * gain[...]).astype(BF16)
    y_s[...] = jnp.zeros_like(y_s)
    db_s[...] = jnp.zeros_like(db_s)

    def hidden_tile(i, _):
        at = pl.ds(pl.multiple_of(i * tile, tile), tile)
        b, gy = b_s[...], gy_ref[...]
        gate = nt(b, w[0, at, :])
        up = nt(b, w[1, at, :])
        d_act = nt(gy, w[2, at, :])
        sig = jax.nn.sigmoid(gate)
        silu = gate * sig
        act = (silu * up).astype(BF16)
        d_gate = (d_act * up * sig * (1.0 + gate * (1.0 - sig))).astype(BF16)
        d_up = (d_act * silu).astype(BF16)
        total[0, at, :] += tn(d_gate, b)
        total[1, at, :] += tn(d_up, b)
        total[2, at, :] += tn(act, gy)
        y_s[...] += nn(act, w[2, at, :])
        db_s[...] += nn(d_gate, w[0, at, :]) + nn(d_up, w[1, at, :])
        return 0

    lax.fori_loop(0, hidden // tile, hidden_tile, 0)
    y_ref[...] = y_s[...].astype(BF16)
    db_ref[...] = db_s[...].astype(BF16)

    @pl.when(step == pl.num_programs(0) - 1)
    def _():
        for k in range(3):
            out_s[k] = total[k].astype(BF16)
            for d in range(pieces):
                store(k, d).start()
        for k in range(3):
            for d in range(pieces):
                store(k, d).wait()


def ffn(x, o, gy, w_out, gain, w, chunk):
    rows, width = x.shape
    pieces, _, part, _ = w.shape
    hidden = pieces * part
    tile = next(t for t in (384, 288, 256, 192, 128, 64, hidden) if hidden % t == 0)
    row_spec = pl.BlockSpec((chunk, width), lambda i: (i, 0))
    return pl.pallas_call(
        functools.partial(ffn_kernel, tile),
        grid=(rows // chunk,),
        out_shape=(
            jax.ShapeDtypeStruct((rows, width), BF16),
            jax.ShapeDtypeStruct((rows, width), BF16),
            jax.ShapeDtypeStruct((pieces, 3, part, width), BF16),
        ),
        in_specs=[row_spec] * 3 + [
            pl.BlockSpec((width, width), lambda i: (0, 0), pipeline_mode=pl.Buffered(1)),
            pl.BlockSpec((1, width), lambda i: (0, 0)),
            pl.BlockSpec(memory_space=pl.ANY),
        ],
        out_specs=(row_spec, row_spec, pl.BlockSpec(memory_space=pl.ANY)),
        scratch_shapes=[
            VMEM((3, hidden, width), BF16),
            VMEM((3, hidden, width), F32),
            VMEM((chunk, width), BF16),
            VMEM((chunk, width), F32),
            VMEM((chunk, width), F32),
            VMEM((3, hidden, width), BF16),
            pltpu.SemaphoreType.DMA((3, pieces)),
        ],
        compiler_params=pltpu.CompilerParams(vmem_limit_bytes=LIMIT),
        name="ffn",
    )(x, o, gy, w_out, gain, w)


def norm_factor(u):
    return lax.rsqrt(jnp.mean(u * u, axis=-1, keepdims=True) + EPS)


def norm_back(u, gain, upstream):
    factor = norm_factor(u)
    unit = u * factor
    weighted = upstream * gain
    back = factor * (weighted - unit * jnp.mean(weighted * unit, axis=-1, keepdims=True))
    return back, jnp.sum(upstream * unit, axis=0)


def place_tables(segment_row, order_row):
    length = segment_row.shape[0]
    docs = jnp.arange(1, MOST_DOCS, dtype=jnp.int32)
    begins = jnp.sum(segment_row[None, :] < docs[:, None], axis=1, dtype=jnp.int32)
    starts = jnp.max(jnp.where(segment_row[None, :] >= docs[:, None], begins[:, None], 0), axis=0)
    blocks = order_row.shape[0]
    ids = jnp.arange(blocks, dtype=jnp.int32)
    inv = jnp.sum(jnp.where(order_row[None, :] == ids[:, None], ids[None, :], 0), axis=1, dtype=jnp.int32)
    first = starts.reshape(blocks, BLOCK)[:, 0] // BLOCK
    lane = jnp.arange(PAIR, dtype=jnp.int32)
    frequency = jnp.exp((lane % (HEAD // 2)).astype(F32) * (-2.0 * math.log(THETA) / HEAD))
    offset = (jnp.arange(length, dtype=jnp.int32) - starts).astype(F32)
    turned = offset[:, None] * frequency[None, :]
    sign = jnp.where(lane % HEAD < HEAD // 2, -1.0, 1.0)
    return inv, first, starts, jnp.cos(turned), jnp.sin(turned) * sign[None, :]


def shards(tokens_in, norm_attn, w_query, w_keyval, gain_query, gain_key, w_out, norm_ffn,
           w_gate, w_up, w_down, cotangent, segments, blocks):
    seq, dp = lax.axis_size("seq"), lax.axis_size("dp")
    me = lax.axis_index("seq")
    rows, width = tokens_in.shape
    total_rows = rows * seq
    mine = KEY_VALUE_HEADS // seq * PAIR
    depth = w_query.shape[0]
    part = w_down.shape[0] // seq

    def my_columns(u):
        return lax.dynamic_slice_in_dim(u, me * mine, mine, 1)

    gain_row = jnp.concatenate([norm_attn, norm_ffn, gain_query, gain_key])
    sizes = (norm_attn.shape[0], norm_ffn.shape[0], gain_query.shape[0], gain_key.shape[0])
    gain_rows = jnp.pad(gain_row[None, :], ((0, 15), (0, 2 * mine - gain_row.shape[0])))
    packed = jnp.concatenate([jnp.concatenate([my_columns(w_query), my_columns(w_keyval)], 1), gain_rows], 0)
    packed = lax.all_gather(packed, "dp", axis=0)
    w_qkv = packed[:, :depth].reshape(width, 2 * mine)
    gains = packed[:, depth].astype(F32)
    g_attn, g_ffn, g_query, g_key = (
        gains[:, sum(sizes[:i]):sum(sizes[:i + 1])].reshape(-1) for i in range(4))
    out_w = lax.all_gather(w_out, "dp", axis=0, tiled=True)

    def my_rows(u):
        return lax.dynamic_slice_in_dim(u, me * part, part, 0)

    ffn_w = jnp.stack([my_rows(w_gate.T), my_rows(w_up.T), my_rows(w_down)])
    ffn_w = lax.all_gather(ffn_w, "dp", axis=0)
    pieces = dp if part % 16 == 0 else 1
    if pieces == 1:
        ffn_w = jnp.moveaxis(ffn_w, 0, 1).reshape(1, 3, dp * part, width)

    inv, first, starts, cos, sin = place_tables(segments[0], blocks[0])
    starts_down = jnp.broadcast_to(starts[:, None], (total_rows, BLOCK))
    starts_across = jnp.broadcast_to(starts.reshape(-1, 1, BLOCK), (total_rows // BLOCK, 8, BLOCK))
    gain_q = jnp.tile(g_query, mine // HEAD)[None, :]
    gain_kv = jnp.tile(jnp.concatenate([g_key, jnp.ones_like(g_key)]), mine // PAIR)[None, :]

    x_all = lax.all_gather(tokens_in, "seq", axis=0, tiled=True)
    gy_all = lax.all_gather(cotangent, "seq", axis=0, tiled=True)
    hidden = x_all.astype(F32)
    a_all = (hidden * norm_factor(hidden) * g_attn).astype(BF16)
    qkv = nn(a_all, w_qkv)
    q_raw, kv_raw = qkv[:, :mine], qkv[:, mine:]
    o, qs, kvs, linv = attend(inv, first, q_raw, kv_raw, cos, sin, starts_down, gain_q, gain_kv)

    o_all = lax.all_gather(o, "seq", axis=1, tiled=True)
    y_part, db_part, ffn_grads = ffn(x_all, o_all, gy_all, out_w, g_ffn[None, :], ffn_w, min(rows, 512))
    d_b = lax.psum_scatter(db_part, "seq", scatter_dimension=0, tiled=True).astype(F32)
    y = lax.psum_scatter(y_part, "seq", scatter_dimension=0, tiled=True).astype(F32)

    if pieces == 1:
        ffn_grads = jnp.moveaxis(ffn_grads.reshape(3, dp, part, width), 1, 0)
    ffn_grads = lax.psum_scatter(ffn_grads, "dp", scatter_dimension=0, tiled=True)[0]
    ffn_grads = lax.all_gather(ffn_grads, "seq", axis=1, tiled=True).astype(F32)

    x_own = tokens_in.astype(F32)
    o_own = lax.dynamic_slice_in_dim(o_all, me * rows, rows, 0)
    x1 = x_own + nn(o_own, out_w)
    output = (x1 + y).astype(BF16)
    d_x1, d_g_ffn = norm_back(x1, g_ffn, d_b)
    d_x1 = d_x1 + cotangent.astype(F32)
    d_y = d_x1.astype(BF16)
    grad_out = tn(o_own, d_y)
    d_o = nt(d_y, out_w).astype(BF16)
    d_o = lax.all_to_all(d_o, "seq", split_axis=1, concat_axis=0, tiled=True)

    dq_raw, dkv_raw, gain_sums = attend_back(
        inv, first, q_raw, kv_raw, cos, sin, starts_across, gain_q, gain_kv, o, d_o, qs, kvs, linv)
    d_qkv = jnp.concatenate([dq_raw, dkv_raw], 1)
    da_part = nt(d_qkv, w_qkv).astype(BF16)
    grad_qkv = tn(a_all, d_qkv)
    d_a = lax.psum_scatter(da_part, "seq", scatter_dimension=0, tiled=True).astype(F32)
    back, d_g_attn = norm_back(x_own, g_attn, d_a)
    grad_tokens = d_x1 + back
    q_sums, k_sums = jnp.sum(gain_sums[:8], 0), jnp.sum(gain_sums[8:], 0)
    d_g_query = jnp.sum(q_sums.reshape(-1, HEAD), 0)
    d_g_key = jnp.sum(k_sums.reshape(-1, PAIR)[:, :HEAD], 0)

    small = jnp.concatenate(
        [u.reshape(dp, -1) for u in (d_g_attn, d_g_ffn, d_g_query, d_g_key)], 1)
    small = jnp.pad(small, ((0, 0), (0, width - small.shape[1])))[:, None, :]
    small = jnp.pad(small, ((0, 0), (0, 15), (0, 0)))
    bundle = jnp.concatenate(
        [grad_qkv.reshape(dp, -1, width), grad_out.reshape(dp, -1, width), small], 1).astype(BF16)
    bundle = lax.psum_scatter(bundle, "dp", scatter_dimension=0, tiled=True)[0]
    bundle = lax.all_gather(bundle, "seq", axis=0).astype(F32)
    n_qkv = depth * 2 * mine // width
    g_qkv = bundle[:, :n_qkv].reshape(seq, depth, 2, mine)
    grad_wq = jnp.moveaxis(g_qkv[:, :, 0], 0, 1).reshape(depth, width)
    grad_wkv = jnp.moveaxis(g_qkv[:, :, 1], 0, 1).reshape(depth, width)
    rest = jnp.sum(bundle[:, n_qkv:], 0)
    grad_wout = rest[:depth]
    tail = rest[depth]
    grads = [tail[sum(sizes[:i]):sum(sizes[:i + 1])] for i in range(4)]
    return (output, grad_tokens, grads[0], grad_wq, grad_wkv, grads[2], grads[3], grad_wout, grads[1],
            ffn_grads[0].T, ffn_grads[1].T, ffn_grads[2])


def solution(mesh):
    rows, cols, row2 = P("dp", None), P(None, "dp"), P(("dp", "seq"), None)
    vec = P("dp")
    return jax.shard_map(
        shards,
        mesh=mesh,
        in_specs=(row2, vec, rows, rows, vec, vec, rows, vec, cols, cols, rows, row2, rows, rows),
        out_specs=(row2, row2, vec, rows, rows, vec, vec, rows, vec, cols, cols, rows),
        check_vma=False,
    )
```

```python
import functools
import math

import jax
import jax.numpy as jnp
from jax import lax
from jax.experimental import pallas as pl
from jax.experimental.pallas import tpu as pltpu
from jax.sharding import PartitionSpec as P

KEY_VALUE_HEADS = 8
HEAD = 64
PAIR = 2 * HEAD
BLOCK = 128
SPAN = 256
EPS = 1e-05
THETA = 1000000.0
MOST_DOCS = 8
F32 = jnp.float32
BF16 = jnp.bfloat16
VMEM = pltpu.VMEM
LIMIT = 66000000


def nn(a, b):
    return lax.dot_general(a, b, (((1,), (0,)), ((), ())), preferred_element_type=F32)


def nt(a, b):
    return lax.dot_general(a, b, (((1,), (1,)), ((), ())), preferred_element_type=F32)


def tn(a, b):
    return lax.dot_general(a, b, (((0,), (0,)), ((), ())), preferred_element_type=F32)


def split_dot(a, b):
    high = a.astype(BF16)
    low = (a - high.astype(F32)).astype(BF16)
    return nn(high, b) + nn(low, b)


def lanes(shape):
    return lax.broadcasted_iota(jnp.int32, shape, len(shape) - 1)


def head_mean(wide):
    row = lax.broadcasted_iota(jnp.int32, (wide, wide), 0) // HEAD
    col = lax.broadcasted_iota(jnp.int32, (wide, wide), 1) // HEAD
    return jnp.where(row == col, 1.0 / HEAD, 0.0).astype(BF16)


def partner(u):
    wide, half = u.shape[-1], HEAD // 2
    front = lanes(u.shape) % HEAD < half
    return jnp.where(front, pltpu.roll(u, wide - half, 1), pltpu.roll(u, half, 1))


def swap_heads(u):
    return pltpu.roll(u, HEAD, 1)


def tile_lanes(u, times):
    return u if times == 1 else jnp.concatenate([u] * times, axis=1)


def attend_kernel(groups, inv, first, q_raw, kv_raw, cos, sin, starts, gain_q, gain_kv,
                  o_ref, qs, kvs, linv, ov):
    blocks = inv.shape[0]
    wide = q_raw.shape[1]
    mean = head_mean(wide)
    low_half = lanes((BLOCK, PAIR)) < HEAD
    is_key = lanes((BLOCK, wide)) % PAIR < HEAD

    def prepare(p, _):
        rows = pl.ds(pl.multiple_of(inv[p] * BLOCK, BLOCK), BLOCK)
        place = pl.ds(pl.multiple_of(p * BLOCK, BLOCK), BLOCK)
        c = tile_lanes(cos[place, :], groups)
        s = tile_lanes(sin[place, :], groups)

        def turned(raw, gain):
            u = raw * lax.rsqrt(split_dot(raw * raw, mean) + EPS) * gain
            return u * c + partner(u) * s

        q = turned(q_raw[rows, :], gain_q[0:1, :]) * (HEAD ** -0.5)
        kv = kv_raw[rows, :]
        kv = jnp.where(is_key, turned(kv, gain_kv[0:1, :]), kv)
        for g in range(groups):
            pair = q[:, g * PAIR:(g + 1) * PAIR]
            qs[g, pl.ds(pl.multiple_of(p * SPAN, SPAN), BLOCK), :] = jnp.where(low_half, pair, 0.0).astype(BF16)
            qs[g, pl.ds(pl.multiple_of(p * SPAN + BLOCK, BLOCK), BLOCK), :] = jnp.where(
                low_half, swap_heads(pair), 0.0).astype(BF16)
            one = kv[:, g * PAIR:(g + 1) * PAIR]
            kvs[g, place, :] = one.astype(BF16)
            ov[g, place, :] = jnp.where(low_half, 1.0, one).astype(BF16)
        return 0

    lax.fori_loop(0, blocks, prepare, 0)
    for g in range(groups):
        kvs[g, blocks * BLOCK:, :] = jnp.zeros((BLOCK, PAIR), BF16)
        ov[g, blocks * BLOCK:, :] = jnp.zeros((BLOCK, PAIR), BF16)

    def one_block(p, _):
        base = p * BLOCK
        row = base + lax.broadcasted_iota(jnp.int32, (BLOCK, SPAN), 0)
        start = tile_lanes(starts[pl.ds(pl.multiple_of(base, BLOCK), BLOCK), :], SPAN // BLOCK)
        begin = first[p]

        def step(i, totals):
            at = pl.multiple_of((begin + 2 * i) * BLOCK, BLOCK)
            col = at + lanes((BLOCK, SPAN))
            allowed = (col >= start) & (col <= row)
            keys = pl.ds(at, SPAN)
            result = []
            for g in range(groups):
                score = nt(qs[g, pl.ds(pl.multiple_of(p * SPAN, SPAN), SPAN), :], kvs[g, keys, :])
                e = jnp.exp(score)
                e = jnp.concatenate([jnp.where(allowed, e[:BLOCK], 0.0), jnp.where(allowed, e[BLOCK:], 0.0)], axis=0)
                result.append(totals[g] + nn(e.astype(BF16), ov[g, keys, :]))
            return tuple(result)

        totals = lax.fori_loop(
            0, (p - begin) // 2 + 1, step, tuple(jnp.zeros((SPAN, PAIR), F32) for _ in range(groups)))
        rows = pl.ds(pl.multiple_of(inv[p] * BLOCK, BLOCK), BLOCK)
        for g in range(groups):
            total = totals[g]
            linv[g, p, :, :] = 1.0 / jnp.transpose(total)[0:8, :]
            one, two = total[:BLOCK], total[BLOCK:]
            o = jnp.where(low_half, swap_heads(one) / one, two / swap_heads(two))
            o_ref[rows, g * PAIR:(g + 1) * PAIR] = o.astype(BF16)
        return 0

    lax.fori_loop(0, blocks, one_block, 0)


def attend(inv, first, q_raw, kv_raw, cos, sin, starts, gain_q, gain_kv):
    rows, wide = q_raw.shape
    groups = wide // PAIR
    blocks = rows // BLOCK
    whole = pl.BlockSpec(memory_space=VMEM)
    return pl.pallas_call(
        functools.partial(attend_kernel, groups),
        out_shape=(
            jax.ShapeDtypeStruct((rows, wide), BF16),
            jax.ShapeDtypeStruct((groups, rows * 2, PAIR), BF16),
            jax.ShapeDtypeStruct((groups, rows + BLOCK, PAIR), BF16),
            jax.ShapeDtypeStruct((groups, blocks, 8, SPAN), F32),
        ),
        in_specs=[pl.BlockSpec(memory_space=pltpu.SMEM)] * 2 + [whole] * 7,
        out_specs=(whole,) * 4,
        scratch_shapes=[VMEM((groups, rows + BLOCK, PAIR), BF16)],
        compiler_params=pltpu.CompilerParams(vmem_limit_bytes=LIMIT),
        name="attend",
    )(inv, first, q_raw, kv_raw, cos, sin, starts, gain_q, gain_kv)


def attend_back_kernel(groups, inv, first, q_raw, kv_raw, cos, sin, starts, gain_q, gain_kv, o_ref, do_ref,
                       qs, kvs, linv, dq_ref, dkv_ref, gains_ref, kt, dkv, dq):
    blocks = inv.shape[0]
    wide = q_raw.shape[1]
    mean = head_mean(wide)
    low_half = lanes((BLOCK, PAIR)) < HEAD
    is_key = lanes((BLOCK, wide)) % PAIR < HEAD
    pick = (lax.broadcasted_iota(jnp.int32, (16, PAIR), 1) // HEAD
            == lax.broadcasted_iota(jnp.int32, (16, PAIR), 0) // 8).astype(BF16)

    dkv[...] = jnp.zeros_like(dkv)

    def turn_keys(p, _):
        place = pl.ds(pl.multiple_of(p * BLOCK, BLOCK), BLOCK)
        for g in range(groups):
            kt[g, :, place] = jnp.transpose(kvs[g, place, :].astype(F32))[:HEAD].astype(BF16)
        return 0

    lax.fori_loop(0, blocks, turn_keys, 0)
    for g in range(groups):
        kt[g, :, blocks * BLOCK:] = jnp.zeros((HEAD, BLOCK), BF16)

    def one_block(p, _):
        base = p * BLOCK
        rows = pl.ds(pl.multiple_of(inv[p] * BLOCK, BLOCK), BLOCK)
        queries = pl.ds(pl.multiple_of(p * SPAN, SPAN), SPAN)
        place_q = base + lanes((SPAN, SPAN)) % BLOCK
        start = jnp.broadcast_to(tile_lanes(starts[p, 0:1, :], 2), (SPAN, SPAN))
        begin = first[p]
        grads, dots = [], []
        for g in range(groups):
            pair = do_ref[rows, g * PAIR:(g + 1) * PAIR].astype(F32)
            grads.append(jnp.concatenate(
                [jnp.where(low_half, 0.0, swap_heads(pair)), jnp.where(low_half, 0.0, pair)], axis=0).astype(BF16))
            prod = pair * o_ref[rows, g * PAIR:(g + 1) * PAIR].astype(F32)
            high = prod.astype(BF16)
            low = (prod - high.astype(F32)).astype(BF16)
            d = nt(pick, high) + nt(pick, low)
            dots.append(jnp.concatenate([d[0:1], d[8:9]], axis=1))

        def step(i, totals):
            at = pl.multiple_of((begin + 2 * i) * BLOCK, BLOCK)
            keys = pl.ds(at, SPAN)
            place_k = at + lax.broadcasted_iota(jnp.int32, (SPAN, SPAN), 0)
            allowed = (place_k >= start) & (place_k <= place_q)
            result = []
            for g in range(groups):
                q = qs[g, queries, :]
                kv = kvs[g, keys, :]
                p_t = jnp.where(allowed, jnp.exp(nt(kv, q)) * linv[g, p, 0:1, :], 0.0)
                ds_t = (p_t * (nt(kv, grads[g]) - dots[g])).astype(BF16)
                dkv[g, keys, :] += nn(ds_t, q) + nn(p_t.astype(BF16), grads[g])
                result.append(totals[g] + nn(kt[g, :, keys], ds_t))
            return tuple(result)

        totals = lax.fori_loop(
            0, (p - begin) // 2 + 1, step, tuple(jnp.zeros((HEAD, SPAN), F32) for _ in range(groups)))
        for g in range(groups):
            total = totals[g]
            stacked = jnp.concatenate([total[:, :BLOCK], total[:, BLOCK:]], axis=0)
            dq[pl.ds(pl.multiple_of(base, BLOCK), BLOCK), g * PAIR:(g + 1) * PAIR] = (
                jnp.transpose(stacked) * (HEAD ** -0.5))
        return 0

    lax.fori_loop(0, blocks, one_block, 0)

    def finish(p, sums):
        rows = pl.ds(pl.multiple_of(inv[p] * BLOCK, BLOCK), BLOCK)
        place = pl.ds(pl.multiple_of(p * BLOCK, BLOCK), BLOCK)
        c = tile_lanes(cos[place, :], groups)
        s = tile_lanes(sin[place, :], groups)

        def back(raw, gain, grad):
            u = grad.astype(BF16).astype(F32)
            u = u * c - partner(u) * s
            factor = lax.rsqrt(split_dot(raw * raw, mean) + EPS)
            n = raw * factor
            term = u * n
            return factor * (u * gain - n * split_dot(term * gain, mean)), term

        dq_raw, q_term = back(q_raw[rows, :], gain_q[0:1, :], dq[place, :])
        dq_ref[rows, :] = dq_raw.astype(BF16)
        grad = jnp.concatenate([dkv[g, place, :] for g in range(groups)], axis=1)
        dk_raw, k_term = back(kv_raw[rows, :], gain_kv[0:1, :], grad)
        dkv_ref[rows, :] = jnp.where(is_key, dk_raw, grad).astype(BF16)

        def folded(term):
            return jnp.sum(term.reshape(BLOCK // 8, 8, wide), axis=0)

        return sums[0] + folded(q_term), sums[1] + folded(k_term)

    zero = jnp.zeros((8, wide), F32)
    sums = lax.fori_loop(0, blocks, finish, (zero, zero))
    gains_ref[0:8, :] = sums[0]
    gains_ref[8:16, :] = sums[1]


def attend_back(inv, first, q_raw, kv_raw, cos, sin, starts, gain_q, gain_kv, o, do, qs, kvs, linv):
    rows, wide = q_raw.shape
    groups = wide // PAIR
    whole = pl.BlockSpec(memory_space=VMEM)
    return pl.pallas_call(
        functools.partial(attend_back_kernel, groups),
        out_shape=(
            jax.ShapeDtypeStruct((rows, wide), BF16),
            jax.ShapeDtypeStruct((rows, wide), BF16),
            jax.ShapeDtypeStruct((16, wide), F32),
        ),
        in_specs=[pl.BlockSpec(memory_space=pltpu.SMEM)] * 2 + [whole] * 12,
        out_specs=(whole,) * 3,
        scratch_shapes=[
            VMEM((groups, HEAD, rows + BLOCK), BF16),
            VMEM((groups, rows + BLOCK, PAIR), F32),
            VMEM((rows, wide), F32),
        ],
        compiler_params=pltpu.CompilerParams(vmem_limit_bytes=LIMIT),
        name="attend_back",
    )(inv, first, q_raw, kv_raw, cos, sin, starts, gain_q, gain_kv, o, do, qs, kvs, linv)


def other(index, bits, count):
    flipped, weight = 0, 1
    while weight < count:
        one, two = (index // weight) % 2, (bits // weight) % 2
        flipped = flipped + weight * (one + two - 2 * one * two)
        weight *= 2
    return flipped


def greet(seq, me, dp=0, here=0):
    barrier = pltpu.get_barrier_semaphore()
    peers = [{"seq": other(me, j, seq)} for j in range(1, seq)]
    if dp:
        peers += [{"dp": other(here, 1, dp)}] + [{"dp": other(here, 2 * t, dp)} for t in range(1, dp // 2)]
    for peer in peers:
        pl.semaphore_signal(barrier, inc=1, device_id=peer, device_id_type=pl.DeviceIdType.MESH)
    pl.semaphore_wait(barrier, len(peers))


def send(source, target, sems, at, peer, axis="seq"):
    return pltpu.make_async_remote_copy(
        src_ref=source, dst_ref=target, send_sem=sems[0].at[at], recv_sem=sems[1].at[at],
        device_id={axis: peer}, device_id_type=pl.DeviceIdType.MESH)


def flips(seq):
    bits = [1 << i for i in range(seq.bit_length() - 1)]
    return bits, bits[::-1]


class Gather:
    def __init__(self, me, seq, own, slots, sems):
        self.me, self.seq, self.own, self.slots, self.sems = me, seq, own, slots, sems
        self.half = own.shape[0] // 2
        self.orders = flips(seq)
        self.arrived = set()
        self.source = {}
        self.items = []
        for step in range(len(self.orders[0])):
            for part in range(2):
                bits = self.orders[part]
                held = [0]
                for bit in bits[:step]:
                    held += [k + bit for k in held]
                for k in held:
                    self.items.append((part, step, k))
                    self.source[part, k + bits[step]] = (part, step, k)

    def copy(self, part, step, k):
        bit = self.orders[part][step]
        rows = pl.ds(part * self.half, self.half)
        source = self.own.at[rows, :] if k == 0 else self.slots.at[k, rows, :]
        return send(source, self.slots.at[k + bit, rows, :], self.sems, (part, step, k), other(self.me, bit, self.seq))

    def begin(self):
        for item in self.items:
            if item[2] == 0:
                self.copy(*item).start()

    def wait(self, part, k):
        if (part, k) not in self.arrived:
            self.arrived.add((part, k))
            self.copy(*self.source[part, k]).wait_recv()

    def forward(self):
        for item in self.items:
            if item[2] != 0:
                self.wait(item[0], item[2])
                self.copy(*item).start()

    def finish(self, k):
        self.wait(0, k)
        self.wait(1, k)

    def drain(self):
        for item in self.items:
            self.copy(*item).wait_send()

    @staticmethod
    def semaphores(seq):
        return pltpu.SemaphoreType.DMA((2, max(seq.bit_length() - 1, 1), seq))


class Spread:
    def __init__(self, here, dp, own, slots, sems):
        self.here, self.dp, self.own, self.slots = here, dp, own, slots
        self.far, self.near = sems[:2], sems[2:]

    def to_far(self, t):
        return send(self.own, self.slots.at[self.here], self.far, t, other(self.here, 2 * t, self.dp), "dp")

    def to_near(self, t):
        owner = other(self.here, 2 * t, self.dp)
        source = self.own if t == 0 else self.slots.at[owner]
        return send(source, self.slots.at[owner], self.near, t, other(self.here, 1, self.dp), "dp")

    def begin(self):
        for t in range(1, self.dp // 2):
            self.to_far(t).start()
        self.to_near(0).start()

    def forward(self):
        for t in range(1, self.dp // 2):
            self.to_far(t).wait_recv()
            self.to_near(t).start()

    def finish(self):
        for t in range(self.dp // 2):
            self.to_near(t).wait_recv()

    def drain(self):
        for t in range(1, self.dp // 2):
            self.to_far(t).wait_send()
        for t in range(self.dp // 2):
            self.to_near(t).wait_send()

    @staticmethod
    def semaphores(dp):
        return [pltpu.SemaphoreType.DMA((dp // 2,))] * 4


def selected(piece, offset, size, owner, wide, period):
    group = offset // PAIR
    lane = lax.broadcasted_iota(jnp.int32, (PAIR, wide), 0) - offset % PAIR
    place = lax.broadcasted_iota(jnp.int32, (PAIR, wide), 1) % period
    hot = (place == lane + owner * size) & (lane >= 0) & (lane < size)
    return nn(piece[:, group * PAIR:(group + 1) * PAIR], hot.astype(BF16))


def project_kernel(seq, dp, sizes, x_ref, pack_ref, x_all, a_all, q_raw, kv_raw, w_ref, g_attn, g_ffn, g_q, g_kv,
                   packs, x_send, x_recv, far_out, far_in, near_out, near_in, own_sem):
    me, here = lax.axis_index("seq"), lax.axis_index("dp")
    rows, width = x_ref.shape
    depth = pack_ref.shape[0] - 16
    mine = q_raw.shape[1]
    gather = Gather(me, seq, x_ref, x_all, (x_send, x_recv))
    pack = Spread(here, dp, pack_ref, packs, (far_out, far_in, near_out, near_in))
    greet(seq, me, dp, here)
    pack.begin()
    gather.begin()
    copies = [pltpu.make_async_copy(x_ref, x_all.at[0], own_sem.at[0]),
              pltpu.make_async_copy(pack_ref, packs.at[here], own_sem.at[1])]
    for copy in copies:
        copy.start()
    pack.forward()
    gather.forward()
    pack.finish()
    copies[1].wait()
    totals = [jnp.zeros((16, width), F32)] * 2 + [jnp.zeros((16, mine), F32)] * 2
    for d in range(dp):
        w_ref[d * depth:(d + 1) * depth, :] = packs[d, :depth, :]
        piece = packs[d, depth:, :]
        for i, period in enumerate((width, width, HEAD, PAIR)):
            totals[i] = totals[i] + selected(piece, sum(sizes[:i]), sizes[i], d, totals[i].shape[1], period)
    gain = totals[0][0:1]
    g_attn[...] = totals[0][:8]
    g_ffn[...] = totals[1][:8]
    g_q[...] = totals[2][:8]
    g_kv[...] = jnp.where(lanes((8, mine)) % PAIR < HEAD, totals[3][:8], 1.0)
    for k in [0] + list(range(1, seq)):
        if k:
            gather.finish(k)
        x = (x_ref[...] if k == 0 else x_all[k]).astype(F32)
        a = (x * lax.rsqrt(jnp.mean(x * x, axis=-1, keepdims=True) + EPS) * gain).astype(BF16)
        a_all[k] = a
        qkv = nn(a, w_ref[...])
        at = pl.ds(pl.multiple_of(other(me, k, seq) * rows, rows), rows)
        q_raw[at, :] = qkv[:, :mine]
        kv_raw[at, :] = qkv[:, mine:]
    copies[0].wait()
    gather.drain()
    pack.drain()


def project(x, packed, seq, dp, sizes):
    rows, width = x.shape
    wide = packed.shape[1]
    mine = wide // 2
    whole = pl.BlockSpec(memory_space=VMEM)
    shape = jax.ShapeDtypeStruct
    dma = pltpu.SemaphoreType.DMA
    return pl.pallas_call(
        functools.partial(project_kernel, seq, dp, sizes),
        out_shape=(
            shape((seq, rows, width), BF16), shape((seq, rows, width), BF16),
            shape((seq * rows, mine), F32), shape((seq * rows, mine), F32),
            shape((width, wide), BF16),
            shape((8, width), F32), shape((8, width), F32), shape((8, mine), F32), shape((8, mine), F32)),
        in_specs=[whole] * 2,
        out_specs=(whole,) * 9,
        scratch_shapes=[VMEM((dp,) + packed.shape, BF16), Gather.semaphores(seq), Gather.semaphores(seq)]
        + Spread.semaphores(dp) + [dma((2,))],
        compiler_params=pltpu.CompilerParams(vmem_limit_bytes=LIMIT, collective_id=0, has_side_effects=True),
        name="project",
    )(x, packed)


def ffn_kernel(seq, tile, *refs):
    refs = list(refs)
    o_ref, x_hbm, gain, w_hbm = refs[:4]
    gy_hbm = refs[4:4 + seq]
    rest = refs[4 + seq:]
    grad_hbm, dx_ref, dy_ref, xy_ref, w_out, o_own = rest[:6]
    y_hbm = [None] + rest[6:5 + seq]
    (w, total, o_buf, x_s, gy_s, b_s, y_s, db_s, x1_s, y_out, db_send, db_recv,
     extra, w_sems, o_send, o_recv, db_out, db_in, in_sems, y_sem, extra_sem) = rest[5 + seq:]
    me = lax.axis_index("seq")
    pieces, _, width = w_hbm.shape
    depth = width // pieces
    part = (w_hbm.shape[1] - depth) // 3
    hidden = pieces * part
    rows = dx_ref.shape[0]
    cols = o_ref.shape[1]

    def load_w(k, d):
        source = w_hbm.at[d, pl.ds(k * part, depth if k == 3 else part), :]
        target = w_out.at[pl.ds(d * depth, depth), :] if k == 3 else w.at[k, pl.ds(d * part, part), :]
        return pltpu.make_async_copy(source, target, w_sems.at[k, d])

    def store_w(k, d):
        return pltpu.make_async_copy(
            w.at[k, pl.ds(d * part, part), :], grad_hbm.at[d, pl.ds(k * part, part), :], w_sems.at[k, d])

    def store_extra(d):
        return pltpu.make_async_copy(extra, grad_hbm.at[d, pl.ds(3 * part, 16), :], extra_sem.at[d])

    def chunk_of(k):
        return pl.ds(pl.multiple_of(other(me, k, seq) * rows, rows), rows)

    def load_x(k, slot):
        return pltpu.make_async_copy(x_hbm.at[k], x_s.at[slot], in_sems.at[0, slot])

    def load_gy(k, slot):
        return pltpu.make_async_copy(gy_hbm[k], gy_s.at[slot], in_sems.at[1, slot])

    def start_inputs(k, slot):
        load_x(k, slot).start()
        for one in range(seq):
            @pl.when(k == one)
            def _():
                load_gy(one, slot).start()

    def store_y(k):
        return pltpu.make_async_copy(y_out, y_hbm[k], y_sem)

    def send_o(k, j):
        peer = other(me, j, seq)
        at = pl.ds(pl.multiple_of(other(peer, k, seq) * rows, rows), rows)
        return send(o_ref.at[at, :], o_buf.at[k, j - 1], (o_send, o_recv), (k, j - 1), peer)

    def send_db(k):
        return send(db_send.at[k - 1], db_recv.at[k - 1], (db_out, db_in), k - 1, other(me, k, seq))

    def out_rows(j):
        return pl.ds(pl.multiple_of(other(me, j, seq) * cols, cols), cols)

    for k in (3, 0, 1, 2):
        for d in range(pieces):
            load_w(k, d).start()
    start_inputs(seq - 1, 0)
    greet(seq, me)
    for k in reversed(range(seq)):
        for j in reversed(range(1, seq)):
            send_o(k, j).start()
    total[...] = jnp.zeros_like(total)
    for k in range(4):
        for d in range(pieces):
            load_w(k, d).wait()

    def one_chunk(i, _):
        k = seq - 1 - i
        slot = i % 2
        load_x(0, slot).wait()
        load_gy(0, slot).wait()

        @pl.when(k > 0)
        def _():
            start_inputs(k - 1, 1 - slot)

        for j in range(1, seq):
            send_o(k, j).wait_recv()
        x1 = x_s[slot].astype(F32) + nn(o_ref[chunk_of(k), :], w_out[out_rows(0), :])
        for j in range(1, seq):
            x1 = x1 + nn(o_buf[k, j - 1], w_out[out_rows(j), :])
        x1_s[...] = x1
        scale = lax.rsqrt(jnp.mean(x1 * x1, axis=-1, keepdims=True) + EPS)
        b_s[...] = (x1 * scale * gain[0:1, :]).astype(BF16)
        y_s[...] = jnp.zeros_like(y_s)
        db_s[...] = jnp.zeros_like(db_s)

        def hidden_tile(t, _):
            at = pl.ds(pl.multiple_of(t * tile, tile), tile)
            b, gy = b_s[...], gy_s[slot]
            gate = nt(b, w[0, at, :])
            up = nt(b, w[1, at, :])
            d_act = nt(gy, w[2, at, :])
            sig = jax.nn.sigmoid(gate)
            silu = gate * sig
            act = (silu * up).astype(BF16)
            d_gate = (d_act * up * sig * (1.0 + gate * (1.0 - sig))).astype(BF16)
            d_up = (d_act * silu).astype(BF16)
            total[0, at, :] += tn(d_gate, b)
            total[1, at, :] += tn(d_up, b)
            total[2, at, :] += tn(act, gy)
            y_s[...] += nn(act, w[2, at, :])
            db_s[...] += nn(d_gate, w[0, at, :]) + nn(d_up, w[1, at, :])
            return 0

        lax.fori_loop(0, hidden // tile, hidden_tile, 0)

        @pl.when(k > 0)
        def _():
            db_send[k - 1] = db_s[...].astype(BF16)
            send_db(k).start()

            @pl.when(i > 0)
            def _():
                store_y(1).wait()

            y_out[...] = y_s[...].astype(BF16)
            for one in range(1, seq):
                @pl.when(k == one)
                def _():
                    store_y(one).start()

        return 0

    lax.fori_loop(0, seq, one_chunk, 0)
    for k in range(3):
        w[k] = total[k].astype(BF16)
        for d in range(pieces):
            store_w(k, d).start()
    xy_ref[...] = x1_s[...] + y_s[...]
    o_own[0] = o_ref[chunk_of(0), :]
    for j in range(1, seq):
        o_own[j] = o_buf[0, j - 1]
    db = db_s[...]
    for k in reversed(range(1, seq)):
        send_db(k).wait_recv()
        db = db + db_recv[k - 1].astype(F32)
    x1 = x1_s[...]
    factor = lax.rsqrt(jnp.mean(x1 * x1, axis=-1, keepdims=True) + EPS)
    unit = x1 * factor
    term = db * unit
    weighted = db * gain[0:1, :]
    back = factor * (weighted - unit * jnp.mean(term * gain[0:1, :], axis=-1, keepdims=True))
    dx = gy_s[(seq - 1) % 2].astype(F32) + back
    dx_ref[...] = dx
    dy_ref[...] = dx.astype(BF16)
    extra[...] = jnp.broadcast_to(jnp.sum(term, axis=0, keepdims=True), (16, width)).astype(BF16)
    for d in range(pieces):
        store_extra(d).start()
    for k in range(1, seq):
        send_db(k).wait_send()
    store_y(1).wait()
    for k in range(seq):
        for j in range(1, seq):
            send_o(k, j).wait_send()
    for d in range(pieces):
        store_extra(d).wait()
        for k in range(3):
            store_w(k, d).wait()


def ffn(o, x, gy, gain, w):
    seq = len(gy)
    all_rows, cols = o.shape
    rows, width = gy[0].shape
    pieces = w.shape[0]
    part = (w.shape[1] - width // pieces) // 3
    hidden = pieces * part
    tile = next(t for t in (384, 288, 256, 192, 128, 64, hidden) if hidden % t == 0)
    whole, far = pl.BlockSpec(memory_space=VMEM), pl.BlockSpec(memory_space=pl.ANY)
    wide, narrow = jax.ShapeDtypeStruct((rows, width), F32), jax.ShapeDtypeStruct((rows, width), BF16)
    dma = pltpu.SemaphoreType.DMA
    return pl.pallas_call(
        functools.partial(ffn_kernel, seq, tile),
        out_shape=(jax.ShapeDtypeStruct((pieces, 3 * part + 16, width), BF16), wide, narrow, wide,
                   jax.ShapeDtypeStruct((width, width), BF16),
                   jax.ShapeDtypeStruct((seq, rows, cols), BF16)) + (narrow,) * (seq - 1),
        in_specs=[whole, far, whole, far] + [far] * seq,
        out_specs=(far,) + (whole,) * 5 + (far,) * (seq - 1),
        scratch_shapes=[
            VMEM((3, hidden, width), BF16),
            VMEM((3, hidden, width), F32),
            VMEM((seq, seq - 1, rows, cols), BF16),
            VMEM((2, rows, width), BF16),
            VMEM((2, rows, width), BF16),
            VMEM((rows, width), BF16),
            VMEM((rows, width), F32),
            VMEM((rows, width), F32),
            VMEM((rows, width), F32),
            VMEM((rows, width), BF16),
            VMEM((seq - 1, rows, width), BF16),
            VMEM((seq - 1, rows, width), BF16),
            VMEM((16, width), BF16),
            dma((4, pieces)), dma((seq, seq - 1)), dma((seq, seq - 1)), dma((seq - 1,)), dma((seq - 1,)),
            dma((2, 2)), dma(()), dma((pieces,)),
        ],
        compiler_params=pltpu.CompilerParams(vmem_limit_bytes=LIMIT, collective_id=1, has_side_effects=True),
        name="ffn",
    )(o, x, gain, w, *gy)


def out_back_kernel(seq, dy_ref, w_out, o_own, do_ref, grad_ref, held, send_sem, recv_sem):
    me = lax.axis_index("seq")
    rows, cols = held.shape[1:]
    mine = pl.ds(pl.multiple_of(me * rows, rows), rows)

    def out_rows(j):
        return pl.ds(pl.multiple_of(other(me, j, seq) * cols, cols), cols)

    def send_do(j):
        return send(held.at[j - 1], do_ref.at[mine, :], (send_sem, recv_sem), j - 1, other(me, j, seq))

    greet(seq, me)
    dy = dy_ref[...]
    for j in reversed(range(1, seq)):
        held[j - 1] = nt(dy, w_out[out_rows(j), :]).astype(BF16)
        send_do(j).start()
    do_ref[mine, :] = nt(dy, w_out[out_rows(0), :]).astype(BF16)
    for j in range(seq):
        grad_ref[out_rows(j), :] = tn(o_own[j], dy).astype(BF16)
    for j in range(1, seq):
        send_do(j).wait_send()
        send_do(j).wait_recv()


def out_back(dy, w_out, o_own):
    seq, rows, cols = o_own.shape
    width = dy.shape[1]
    whole = pl.BlockSpec(memory_space=VMEM)
    dma = pltpu.SemaphoreType.DMA
    return pl.pallas_call(
        functools.partial(out_back_kernel, seq),
        out_shape=(jax.ShapeDtypeStruct((seq * rows, cols), BF16), jax.ShapeDtypeStruct((width, width), BF16)),
        in_specs=[whole] * 3,
        out_specs=(whole,) * 2,
        scratch_shapes=[VMEM((seq - 1, rows, cols), BF16), dma((seq - 1,)), dma((seq - 1,))],
        compiler_params=pltpu.CompilerParams(vmem_limit_bytes=LIMIT, collective_id=2, has_side_effects=True),
        name="out_back",
    )(dy, w_out, o_own)


class Reduce:
    def __init__(self, here, dp, pieces, near, out, far, sems):
        self.here, self.dp, self.pieces, self.near, self.out, self.far = here, dp, pieces, near, out, far
        self.sems = sems

    def to_near(self, t):
        mate = other(self.here, 1, self.dp)
        return send(self.pieces.at[other(mate, 2 * t, self.dp)], self.near.at[t], self.sems[2:], t, mate, "dp")

    def to_far(self, t):
        return send(self.out.at[t - 1], self.far.at[t - 1], self.sems[:2], t, other(self.here, 2 * t, self.dp), "dp")

    def begin(self):
        for t in reversed(range(self.dp // 2)):
            self.to_near(t).start()

    def pair(self, t):
        return self.pieces[other(self.here, 2 * t, self.dp)].astype(F32) + self.near[t].astype(F32)

    def middle(self):
        for t in reversed(range(1, self.dp // 2)):
            self.to_near(t).wait_recv()
            self.out[t - 1] = self.pair(t).astype(BF16)
            self.to_far(t).start()

    def finish(self):
        self.to_near(0).wait_recv()
        total = self.pair(0)
        for t in range(1, self.dp // 2):
            self.to_far(t).wait_recv()
            total = total + self.far[t - 1].astype(F32)
        return total

    def drain(self):
        for t in range(self.dp // 2):
            self.to_near(t).wait_send()
        for t in range(1, self.dp // 2):
            self.to_far(t).wait_send()

    @staticmethod
    def scratch(dp, rows, wide):
        return [VMEM((dp // 2, rows, wide), BF16)] + [VMEM((dp // 2 - 1, rows, wide), BF16)] * 2

    @staticmethod
    def semaphores(dp):
        return [pltpu.SemaphoreType.DMA((dp // 2,))] * 4


def project_back_kernel(seq, dp, *refs):
    refs = list(refs)
    dq, dkv, gains, a_all, w, grad_out, x_ref, dx_ref, g_attn, xy_ref = refs[:10]
    y_parts = refs[10:9 + seq]
    (grad_x, out_ref, gwq_ref, gwkv_ref, gwo_ref, gain_out, acc, da, arrived, pieces, results, sums, sum_in,
     q_near, q_out, q_far, o_near, o_out, o_far, rs_out, rs_in, q1, q2, q3, q4, o1, o2, o3, o4,
     all_out, all_in) = refs[9 + seq:]
    me, here = lax.axis_index("seq"), lax.axis_index("dp")
    rows, width = x_ref.shape
    mine = dq.shape[1]
    depth = grad_out.shape[1]
    half = rows // 2
    orders = flips(seq)
    red_q = Reduce(here, dp, pieces, q_near, q_out, q_far, (q1, q2, q3, q4))
    red_o = Reduce(here, dp, grad_out, o_near, o_out, o_far, (o1, o2, o3, o4))

    def chunk(k):
        return pl.ds(pl.multiple_of(other(me, k, seq) * rows, rows), rows)

    def pass_on(part, step, k):
        return send(acc.at[k, pl.ds(part * half, half), :], arrived.at[part, k - 1], (rs_out, rs_in),
                    (part, step, k), other(me, orders[part][step], seq))

    def sent_at(part, step):
        before = sum(orders[part][:step])
        return [k for k in range(1, seq) if k & orders[part][step] and not k & before]

    def to_all(j):
        peer = other(me, j, seq)
        return [send(results.at[me], results.at[me], (all_out, all_in), (0, j - 1), peer),
                send(sums, sum_in.at[j - 1], (all_out, all_in), (1, j - 1), peer)]

    def partial_da(k):
        return nt(dq[chunk(k), :], w[:, :mine]) + nt(dkv[chunk(k), :], w[:, mine:])

    greet(seq, me, dp, here)
    red_o.begin()
    for k in reversed(range(1, seq)):
        acc[k] = partial_da(k).astype(BF16)
        for part in range(2):
            if k in sent_at(part, 0):
                pass_on(part, 0, k).start()
    da[...] = partial_da(0)
    red_o.middle()
    for d in range(2):
        grads = dq if d == 0 else dkv
        total = tn(a_all[0], grads[chunk(0), :])
        for k in range(1, seq):
            total = total + tn(a_all[k], grads[chunk(k), :])
        pieces[:, :depth, d * mine:(d + 1) * mine] = total.astype(BF16).reshape(dp, depth, mine)
        sum8 = jnp.sum(gains[8 * d:8 * d + 8, :], axis=0, keepdims=True)
        pieces[:, depth:, d * mine:(d + 1) * mine] = jnp.broadcast_to(sum8[None], (dp, 16, mine)).astype(BF16)
    red_q.begin()
    out = xy_ref[...]
    for y in y_parts:
        out = out + y[...].astype(F32)
    out_ref[...] = out.astype(BF16)
    red_q.middle()
    for step in range(len(orders[0])):
        for part in range(2):
            at = pl.ds(part * half, half)
            for k in sent_at(part, step):
                pass_on(part, step, k).wait_recv()
                target = k - orders[part][step]
                if target == 0:
                    da[at, :] += arrived[part, k - 1].astype(F32)
                else:
                    acc[target, at, :] = (acc[target, at, :].astype(F32) + arrived[part, k - 1].astype(F32)).astype(BF16)
            if step + 1 < len(orders[0]):
                for k in sent_at(part, step + 1):
                    pass_on(part, step + 1, k).start()
        if step == 0:
            sum_o = red_o.finish()
            sums[...] = sum_o.astype(BF16)
            results[me] = red_q.finish().astype(BF16)
            for j in reversed(range(1, seq)):
                for copy in to_all(j):
                    copy.start()
    x = x_ref[...].astype(F32)
    factor = lax.rsqrt(jnp.mean(x * x, axis=-1, keepdims=True) + EPS)
    unit = x * factor
    weighted = da[...] * g_attn[0:1, :]
    grad_x[...] = dx_ref[...] + factor * (weighted - unit * jnp.mean(weighted * unit, axis=-1, keepdims=True))
    gwo = sums[...].astype(F32)
    for j in range(1, seq):
        for copy in to_all(j):
            copy.wait_recv()
        gwo = gwo + sum_in[j - 1].astype(F32)
    gwo_ref[...] = gwo
    gain_total = jnp.zeros((16, 2 * mine), F32)
    for j in range(seq):
        gwq_ref[:, j * mine:(j + 1) * mine] = results[j, :depth, :mine].astype(F32)
        gwkv_ref[:, j * mine:(j + 1) * mine] = results[j, :depth, mine:].astype(F32)
        gain_total = gain_total + results[j, depth:, :].astype(F32)
    gain_out[...] = gain_total
    for j in range(1, seq):
        for copy in to_all(j):
            copy.wait_send()
    for part in range(2):
        for step in range(len(orders[0])):
            for k in sent_at(part, step):
                pass_on(part, step, k).wait_send()
    red_q.drain()
    red_o.drain()


def project_back(dq, dkv, gains, a_all, w_qkv, grad_out, x, dx, g_attn, xy, y_parts):
    seq, rows, width = a_all.shape
    dp, depth, _ = grad_out.shape
    mine = dq.shape[1]
    whole = pl.BlockSpec(memory_space=VMEM)
    shape = jax.ShapeDtypeStruct
    dma = pltpu.SemaphoreType.DMA
    steps = seq.bit_length() - 1
    return pl.pallas_call(
        functools.partial(project_back_kernel, seq, dp),
        out_shape=(shape((rows, width), F32), shape((rows, width), BF16), shape((depth, seq * mine), F32),
                   shape((depth, seq * mine), F32), shape((depth, width), F32), shape((16, 2 * mine), F32)),
        in_specs=[whole] * (9 + seq),
        out_specs=(whole,) * 6,
        scratch_shapes=[
            VMEM((seq, rows, width), BF16),
            VMEM((rows, width), F32),
            VMEM((2, seq - 1, rows // 2, width), BF16),
            VMEM((dp, depth + 16, 2 * mine), BF16),
            VMEM((seq, depth + 16, 2 * mine), BF16),
            VMEM((depth, width), BF16),
            VMEM((seq - 1, depth, width), BF16),
            *Reduce.scratch(dp, depth + 16, 2 * mine), *Reduce.scratch(dp, depth, width),
            dma((2, steps, seq)), dma((2, steps, seq)),
            *Reduce.semaphores(dp), *Reduce.semaphores(dp), dma((2, seq - 1)), dma((2, seq - 1)),
        ],
        compiler_params=pltpu.CompilerParams(vmem_limit_bytes=LIMIT, collective_id=3, has_side_effects=True),
        name="project_back",
    )(dq, dkv, gains, a_all, w_qkv, grad_out, x, dx, g_attn, xy, *y_parts)


def share_kernel(seq, own, grads_ref, extra_ref, slots, send_sem, recv_sem):
    me = lax.axis_index("seq")
    gather = Gather(me, seq, own, slots, (send_sem, recv_sem))
    part = grads_ref.shape[2]
    greet(seq, me)
    gather.begin()
    extra = own[3 * part:, :].astype(F32)
    for k in range(3):
        grads_ref[k, me] = own[k * part:(k + 1) * part, :].astype(F32)
    gather.forward()
    for j in range(1, seq):
        gather.finish(j)
        for k in range(3):
            grads_ref[k, other(me, j, seq)] = slots[j, k * part:(k + 1) * part, :].astype(F32)
        extra = extra + slots[j, 3 * part:, :].astype(F32)
    extra_ref[...] = extra
    gather.drain()


def share(own, seq, part):
    rows, width = own.shape
    spare = rows - 3 * part
    whole = pl.BlockSpec(memory_space=VMEM)
    shape = jax.ShapeDtypeStruct
    return pl.pallas_call(
        functools.partial(share_kernel, seq),
        out_shape=(shape((3, seq, part, width), F32), shape((spare, width), F32)),
        in_specs=[whole],
        out_specs=(whole,) * 2,
        scratch_shapes=[VMEM((seq, rows, width), BF16), Gather.semaphores(seq), Gather.semaphores(seq)],
        compiler_params=pltpu.CompilerParams(vmem_limit_bytes=LIMIT, collective_id=4, has_side_effects=True),
        name="share",
    )(own)


def exchanged(u, bits, seq):
    return lax.ppermute(u, "seq", [(i, i ^ bits) for i in range(seq)])


def place_tables(segment_row, order_row):
    length = segment_row.shape[0]
    docs = jnp.arange(1, MOST_DOCS, dtype=jnp.int32)
    begins = jnp.sum(segment_row[None, :] < docs[:, None], axis=1, dtype=jnp.int32)
    starts = jnp.max(jnp.where(segment_row[None, :] >= docs[:, None], begins[:, None], 0), axis=0)
    blocks = order_row.shape[0]
    ids = jnp.arange(blocks, dtype=jnp.int32)
    inv = jnp.sum(jnp.where(order_row[None, :] == ids[:, None], ids[None, :], 0), axis=1, dtype=jnp.int32)
    first = starts.reshape(blocks, BLOCK)[:, 0] // BLOCK
    lane = jnp.arange(PAIR, dtype=jnp.int32)
    frequency = jnp.exp((lane % (HEAD // 2)).astype(F32) * (-2.0 * math.log(THETA) / HEAD))
    offset = (jnp.arange(length, dtype=jnp.int32) - starts).astype(F32)
    turned = offset[:, None] * frequency[None, :]
    sign = jnp.where(lane % HEAD < HEAD // 2, -1.0, 1.0)
    return inv, first, starts, jnp.cos(turned), jnp.sin(turned) * sign[None, :]


def shards(tokens_in, norm_attn, w_query, w_keyval, gain_query, gain_key, w_out, norm_ffn,
           w_gate, w_up, w_down, cotangent, segments, blocks):
    seq, dp = lax.axis_size("seq"), lax.axis_size("dp")
    me = lax.axis_index("seq")
    rows, width = tokens_in.shape
    total_rows = rows * seq
    mine = KEY_VALUE_HEADS // seq * PAIR
    depth = w_query.shape[0]
    part = w_down.shape[0] // seq

    def my_columns(u):
        return lax.dynamic_slice_in_dim(u, me * mine, mine, 1)

    gain_row = jnp.concatenate([norm_attn, norm_ffn, gain_query, gain_key])
    sizes = (norm_attn.shape[0], norm_ffn.shape[0], gain_query.shape[0], gain_key.shape[0])
    gain_rows = jnp.pad(gain_row[None, :], ((0, 15), (0, 2 * mine - gain_row.shape[0])))
    packed = jnp.concatenate([jnp.concatenate([my_columns(w_query), my_columns(w_keyval)], 1), gain_rows], 0)
    def my_rows(u):
        return lax.dynamic_slice_in_dim(u, me * part, part, 0)

    ffn_w = jnp.concatenate([my_rows(w_gate.T), my_rows(w_up.T), my_rows(w_down), w_out])
    ffn_w = lax.all_gather(ffn_w, "dp", axis=0)
    in_pieces = part % 16 == 0
    if not in_pieces:
        body = jnp.moveaxis(ffn_w[:, :3 * part].reshape(dp, 3, part, width), 0, 1)
        ffn_w = jnp.concatenate([body.reshape(-1, width), ffn_w[:, 3 * part:].reshape(-1, width)])[None]

    inv, first, starts, cos, sin = place_tables(segments[0], blocks[0])
    starts_down = jnp.broadcast_to(starts[:, None], (total_rows, BLOCK))
    starts_across = jnp.broadcast_to(starts.reshape(-1, 1, BLOCK), (total_rows // BLOCK, 8, BLOCK))
    x_all, a_all, q_raw, kv_raw, w_qkv, g_attn, g_ffn, gain_q, gain_kv = project(
        tokens_in, packed, seq, dp, sizes)
    gy, q_raw = lax.optimization_barrier((cotangent, q_raw))
    gy_all = [gy] + [exchanged(gy, k, seq) for k in range(1, seq)]
    o, qs, kvs, linv = attend(inv, first, q_raw, kv_raw, cos, sin, starts_down, gain_q, gain_kv)

    ffn_grads, d_x1, d_y, x1_y, out_w, o_own, *y_parts = ffn(o, x_all, gy_all, g_ffn, ffn_w)
    if not in_pieces:
        extra = jnp.broadcast_to(ffn_grads[0, None, -16:], (dp, 16, width))
        body = jnp.moveaxis(ffn_grads[0, :-16].reshape(3, dp, part, width), 1, 0)
        ffn_grads = jnp.concatenate([body.reshape(dp, 3 * part, width), extra], 1)
        ffn_grads = jnp.pad(ffn_grads, ((0, 0), (0, -ffn_grads.shape[1] % 32), (0, 0)))
    ffn_grads = lax.psum_scatter(ffn_grads, "dp", scatter_dimension=0, tiled=True)[0]

    d_o, grad_out = out_back(d_y, out_w, o_own)
    d_o, y_parts = lax.optimization_barrier((d_o, y_parts))
    y_parts = [exchanged(y_parts[k - 1], k, seq) for k in range(1, seq)]
    dq_raw, dkv_raw, gain_sums = attend_back(
        inv, first, q_raw, kv_raw, cos, sin, starts_across, gain_q, gain_kv, o, d_o, qs, kvs, linv)
    grad_tokens, output, grad_wq, grad_wkv, grad_wout, gain_sums = project_back(
        dq_raw, dkv_raw, gain_sums, a_all, w_qkv, grad_out.reshape(dp, depth, width), tokens_in, d_x1, g_attn,
        x1_y, y_parts)
    ffn_grads, extra = share(ffn_grads, seq, part)
    ffn_grads = ffn_grads.reshape(3, seq * part, width)

    here = lax.axis_index("dp")

    def owned(vector, size):
        return lax.dynamic_slice_in_dim(vector, here * size, size)

    d_g_ffn = owned(extra[0], sizes[1])
    d_g_query = owned(jnp.sum(gain_sums[0, :mine].reshape(-1, HEAD), 0), sizes[2])
    d_g_key = owned(jnp.sum(gain_sums[0, mine:].reshape(-1, PAIR)[:, :HEAD], 0), sizes[3])
    d_g_attn = jnp.sum(grad_wq * w_query.astype(F32) + grad_wkv * w_keyval.astype(F32), axis=1)
    d_g_attn = d_g_attn / norm_attn.astype(F32)
    return (output, grad_tokens, d_g_attn, grad_wq, grad_wkv, d_g_query, d_g_key, grad_wout, d_g_ffn,
            ffn_grads[0].T, ffn_grads[1].T, ffn_grads[2])


def solution(mesh):
    rows, cols, row2 = P("dp", None), P(None, "dp"), P(("dp", "seq"), None)
    vec = P("dp")
    return jax.shard_map(
        shards,
        mesh=mesh,
        in_specs=(row2, vec, rows, rows, vec, vec, rows, vec, cols, cols, rows, row2, rows, rows),
        out_specs=(row2, row2, vec, rows, rows, vec, vec, rows, vec, cols, cols, rows),
        check_vma=False,
    )
```

```python
import functools
import math

import jax
import jax.numpy as jnp
from jax import lax
from jax.experimental import pallas as pl
from jax.experimental.pallas import tpu as pltpu
from jax.sharding import PartitionSpec as P

KEY_VALUE_HEADS = 8
HEAD = 64
PAIR = 2 * HEAD
BLOCK = 128
SPAN = 256
EPS = 1e-05
THETA = 1000000.0
MOST_DOCS = 8
F32 = jnp.float32
BF16 = jnp.bfloat16
VMEM = pltpu.VMEM
LIMIT = 66000000


def nn(a, b):
    return lax.dot_general(a, b, (((1,), (0,)), ((), ())), preferred_element_type=F32)


def nt(a, b):
    return lax.dot_general(a, b, (((1,), (1,)), ((), ())), preferred_element_type=F32)


def tn(a, b):
    return lax.dot_general(a, b, (((0,), (0,)), ((), ())), preferred_element_type=F32)


def split_dot(a, b):
    high = a.astype(BF16)
    low = (a - high.astype(F32)).astype(BF16)
    return nn(high, b) + nn(low, b)


def lanes(shape):
    return lax.broadcasted_iota(jnp.int32, shape, len(shape) - 1)


def head_mean(wide):
    row = lax.broadcasted_iota(jnp.int32, (wide, wide), 0) // HEAD
    col = lax.broadcasted_iota(jnp.int32, (wide, wide), 1) // HEAD
    return jnp.where(row == col, 1.0 / HEAD, 0.0).astype(BF16)


def partner(u):
    wide, half = u.shape[-1], HEAD // 2
    front = lanes(u.shape) % HEAD < half
    return jnp.where(front, pltpu.roll(u, wide - half, 1), pltpu.roll(u, half, 1))


def swap_heads(u):
    return pltpu.roll(u, HEAD, 1)


def tile_lanes(u, times):
    return u if times == 1 else jnp.concatenate([u] * times, axis=1)


def attend_kernel(groups, inv, first, q_raw, kv_raw, cos, sin, starts, gain_q, gain_kv,
                  o_ref, qs, kvs, linv, ov):
    blocks = inv.shape[0]
    wide = q_raw.shape[1]
    mean = head_mean(wide)
    low_half = lanes((BLOCK, PAIR)) < HEAD
    is_key = lanes((BLOCK, wide)) % PAIR < HEAD

    def prepare(p, _):
        rows = pl.ds(pl.multiple_of(inv[p] * BLOCK, BLOCK), BLOCK)
        place = pl.ds(pl.multiple_of(p * BLOCK, BLOCK), BLOCK)
        c = tile_lanes(cos[place, :], groups)
        s = tile_lanes(sin[place, :], groups)

        def turned(raw, gain):
            u = raw * lax.rsqrt(split_dot(raw * raw, mean) + EPS) * gain
            return u * c + partner(u) * s

        q = turned(q_raw[rows, :], gain_q[0:1, :]) * (HEAD ** -0.5)
        kv = kv_raw[rows, :]
        kv = jnp.where(is_key, turned(kv, gain_kv[0:1, :]), kv)
        for g in range(groups):
            pair = q[:, g * PAIR:(g + 1) * PAIR]
            qs[g, pl.ds(pl.multiple_of(p * SPAN, SPAN), BLOCK), :] = jnp.where(low_half, pair, 0.0).astype(BF16)
            qs[g, pl.ds(pl.multiple_of(p * SPAN + BLOCK, BLOCK), BLOCK), :] = jnp.where(
                low_half, swap_heads(pair), 0.0).astype(BF16)
            one = kv[:, g * PAIR:(g + 1) * PAIR]
            kvs[g, place, :] = one.astype(BF16)
            ov[g, place, :] = jnp.where(low_half, 1.0, one).astype(BF16)
        return 0

    lax.fori_loop(0, blocks, prepare, 0)
    for g in range(groups):
        kvs[g, blocks * BLOCK:, :] = jnp.zeros((BLOCK, PAIR), BF16)
        ov[g, blocks * BLOCK:, :] = jnp.zeros((BLOCK, PAIR), BF16)

    def one_block(p, _):
        base = p * BLOCK
        row = base + lax.broadcasted_iota(jnp.int32, (BLOCK, SPAN), 0)
        start = jnp.transpose(jnp.broadcast_to(starts[pl.ds(p, 1), :].astype(F32), (BLOCK, BLOCK)))
        start = tile_lanes(start.astype(jnp.int32), SPAN // BLOCK)
        begin = first[p]

        def step(i, totals):
            at = pl.multiple_of((begin + 2 * i) * BLOCK, BLOCK)
            col = at + lanes((BLOCK, SPAN))
            allowed = (col >= start) & (col <= row)
            keys = pl.ds(at, SPAN)
            result = []
            for g in range(groups):
                score = nt(qs[g, pl.ds(pl.multiple_of(p * SPAN, SPAN), SPAN), :], kvs[g, keys, :])
                e = jnp.exp(score)
                e = jnp.concatenate([jnp.where(allowed, e[:BLOCK], 0.0), jnp.where(allowed, e[BLOCK:], 0.0)], axis=0)
                result.append(totals[g] + nn(e.astype(BF16), ov[g, keys, :]))
            return tuple(result)

        totals = lax.fori_loop(
            0, (p - begin) // 2 + 1, step, tuple(jnp.zeros((SPAN, PAIR), F32) for _ in range(groups)))
        rows = pl.ds(pl.multiple_of(inv[p] * BLOCK, BLOCK), BLOCK)
        for g in range(groups):
            total = totals[g]
            linv[g, p, :, :] = 1.0 / jnp.transpose(total)[0:8, :]
            one, two = total[:BLOCK], total[BLOCK:]
            o = jnp.where(low_half, swap_heads(one) / one, two / swap_heads(two))
            o_ref[rows, g * PAIR:(g + 1) * PAIR] = o.astype(BF16)
        return 0

    lax.fori_loop(0, blocks, one_block, 0)


def attend(inv, first, q_raw, kv_raw, cos, sin, starts, gain_q, gain_kv):
    rows, wide = q_raw.shape
    groups = wide // PAIR
    blocks = rows // BLOCK
    whole = pl.BlockSpec(memory_space=VMEM)
    return pl.pallas_call(
        functools.partial(attend_kernel, groups),
        out_shape=(
            jax.ShapeDtypeStruct((rows, wide), BF16),
            jax.ShapeDtypeStruct((groups, rows * 2, PAIR), BF16),
            jax.ShapeDtypeStruct((groups, rows + BLOCK, PAIR), BF16),
            jax.ShapeDtypeStruct((groups, blocks, 8, SPAN), F32),
        ),
        in_specs=[pl.BlockSpec(memory_space=pltpu.SMEM)] * 2 + [whole] * 7,
        out_specs=(whole,) * 4,
        scratch_shapes=[VMEM((groups, rows + BLOCK, PAIR), BF16)],
        compiler_params=pltpu.CompilerParams(vmem_limit_bytes=LIMIT),
        name="attend",
    )(inv, first, q_raw, kv_raw, cos, sin, starts, gain_q, gain_kv)


def attend_back_kernel(groups, inv, first, q_raw, kv_raw, cos, sin, starts, gain_q, gain_kv, o_ref, do_ref,
                       qs, kvs, linv, dq_ref, dkv_ref, gains_ref, kt, dkv, dq):
    blocks = inv.shape[0]
    wide = q_raw.shape[1]
    mean = head_mean(wide)
    low_half = lanes((BLOCK, PAIR)) < HEAD
    is_key = lanes((BLOCK, wide)) % PAIR < HEAD
    pick = (lax.broadcasted_iota(jnp.int32, (16, PAIR), 1) // HEAD
            == lax.broadcasted_iota(jnp.int32, (16, PAIR), 0) // 8).astype(BF16)

    dkv[...] = jnp.zeros_like(dkv)

    def turn_keys(p, _):
        place = pl.ds(pl.multiple_of(p * BLOCK, BLOCK), BLOCK)
        for g in range(groups):
            kt[g, :, place] = jnp.transpose(kvs[g, place, :].astype(F32))[:HEAD].astype(BF16)
        return 0

    lax.fori_loop(0, blocks, turn_keys, 0)
    for g in range(groups):
        kt[g, :, blocks * BLOCK:] = jnp.zeros((HEAD, BLOCK), BF16)

    def one_block(p, _):
        base = p * BLOCK
        rows = pl.ds(pl.multiple_of(inv[p] * BLOCK, BLOCK), BLOCK)
        queries = pl.ds(pl.multiple_of(p * SPAN, SPAN), SPAN)
        place_q = base + lanes((SPAN, SPAN)) % BLOCK
        start = jnp.broadcast_to(tile_lanes(starts[pl.ds(p, 1), :], 2), (SPAN, SPAN))
        begin = first[p]
        grads, dots = [], []
        for g in range(groups):
            pair = do_ref[rows, g * PAIR:(g + 1) * PAIR].astype(F32)
            grads.append(jnp.concatenate(
                [jnp.where(low_half, 0.0, swap_heads(pair)), jnp.where(low_half, 0.0, pair)], axis=0).astype(BF16))
            prod = pair * o_ref[rows, g * PAIR:(g + 1) * PAIR].astype(F32)
            high = prod.astype(BF16)
            low = (prod - high.astype(F32)).astype(BF16)
            d = nt(pick, high) + nt(pick, low)
            dots.append(jnp.concatenate([d[0:1], d[8:9]], axis=1))

        def step(i, totals):
            at = pl.multiple_of((begin + 2 * i) * BLOCK, BLOCK)
            keys = pl.ds(at, SPAN)
            place_k = at + lax.broadcasted_iota(jnp.int32, (SPAN, SPAN), 0)
            allowed = (place_k >= start) & (place_k <= place_q)
            result = []
            for g in range(groups):
                q = qs[g, queries, :]
                kv = kvs[g, keys, :]
                p_t = jnp.where(allowed, jnp.exp(nt(kv, q)) * linv[g, p, 0:1, :], 0.0)
                ds_t = (p_t * (nt(kv, grads[g]) - dots[g])).astype(BF16)
                dkv[g, keys, :] += nn(ds_t, q) + nn(p_t.astype(BF16), grads[g])
                result.append(totals[g] + nn(kt[g, :, keys], ds_t))
            return tuple(result)

        totals = lax.fori_loop(
            0, (p - begin) // 2 + 1, step, tuple(jnp.zeros((HEAD, SPAN), F32) for _ in range(groups)))
        for g in range(groups):
            total = totals[g]
            stacked = jnp.concatenate([total[:, :BLOCK], total[:, BLOCK:]], axis=0)
            dq[pl.ds(pl.multiple_of(base, BLOCK), BLOCK), g * PAIR:(g + 1) * PAIR] = (
                jnp.transpose(stacked) * (HEAD ** -0.5))
        return 0

    lax.fori_loop(0, blocks, one_block, 0)

    def finish(p, sums):
        rows = pl.ds(pl.multiple_of(inv[p] * BLOCK, BLOCK), BLOCK)
        place = pl.ds(pl.multiple_of(p * BLOCK, BLOCK), BLOCK)
        c = tile_lanes(cos[place, :], groups)
        s = tile_lanes(sin[place, :], groups)

        def back(raw, gain, grad):
            u = grad.astype(BF16).astype(F32)
            u = u * c - partner(u) * s
            factor = lax.rsqrt(split_dot(raw * raw, mean) + EPS)
            n = raw * factor
            term = u * n
            return factor * (u * gain - n * split_dot(term * gain, mean)), term

        dq_raw, q_term = back(q_raw[rows, :], gain_q[0:1, :], dq[place, :])
        dq_ref[rows, :] = dq_raw.astype(BF16)
        grad = jnp.concatenate([dkv[g, place, :] for g in range(groups)], axis=1)
        dk_raw, k_term = back(kv_raw[rows, :], gain_kv[0:1, :], grad)
        dkv_ref[rows, :] = jnp.where(is_key, dk_raw, grad).astype(BF16)

        def folded(term):
            return jnp.sum(term.reshape(BLOCK // 8, 8, wide), axis=0)

        return sums[0] + folded(q_term), sums[1] + folded(k_term)

    zero = jnp.zeros((8, wide), F32)
    sums = lax.fori_loop(0, blocks, finish, (zero, zero))
    gains_ref[0:8, :] = sums[0]
    gains_ref[8:16, :] = sums[1]


def attend_back(inv, first, q_raw, kv_raw, cos, sin, starts, gain_q, gain_kv, o, do, qs, kvs, linv):
    rows, wide = q_raw.shape
    groups = wide // PAIR
    whole = pl.BlockSpec(memory_space=VMEM)
    return pl.pallas_call(
        functools.partial(attend_back_kernel, groups),
        out_shape=(
            jax.ShapeDtypeStruct((rows, wide), BF16),
            jax.ShapeDtypeStruct((rows, wide), BF16),
            jax.ShapeDtypeStruct((16, wide), F32),
        ),
        in_specs=[pl.BlockSpec(memory_space=pltpu.SMEM)] * 2 + [whole] * 12,
        out_specs=(whole,) * 3,
        scratch_shapes=[
            VMEM((groups, HEAD, rows + BLOCK), BF16),
            VMEM((groups, rows + BLOCK, PAIR), F32),
            VMEM((rows, wide), F32),
        ],
        compiler_params=pltpu.CompilerParams(vmem_limit_bytes=LIMIT),
        name="attend_back",
    )(inv, first, q_raw, kv_raw, cos, sin, starts, gain_q, gain_kv, o, do, qs, kvs, linv)


def other(index, bits, count):
    flipped, weight = 0, 1
    while weight < count:
        one, two = (index // weight) % 2, (bits // weight) % 2
        flipped = flipped + weight * (one + two - 2 * one * two)
        weight *= 2
    return flipped


def greet(seq, me, dp=0, here=0):
    barrier = pltpu.get_barrier_semaphore()
    peers = [{"seq": other(me, j, seq)} for j in range(1, seq)]
    if dp:
        peers += [{"dp": other(here, 1, dp)}] + [{"dp": other(here, 2 * t, dp)} for t in range(1, dp // 2)]
    for peer in peers:
        pl.semaphore_signal(barrier, inc=1, device_id=peer, device_id_type=pl.DeviceIdType.MESH)
    pl.semaphore_wait(barrier, len(peers))


def send(source, target, sems, at, peer, axis="seq"):
    return pltpu.make_async_remote_copy(
        src_ref=source, dst_ref=target, send_sem=sems[0].at[at], recv_sem=sems[1].at[at],
        device_id={axis: peer}, device_id_type=pl.DeviceIdType.MESH)


def flips(seq):
    bits = [1 << i for i in range(seq.bit_length() - 1)]
    return bits, bits[::-1]


class Gather:
    def __init__(self, me, seq, own, slots, sems):
        self.me, self.seq, self.own, self.slots, self.sems = me, seq, own, slots, sems
        self.half = own.shape[0] // 2
        self.orders = flips(seq)
        self.arrived = set()
        self.source = {}
        self.items = []
        for step in range(len(self.orders[0])):
            for part in range(2):
                bits = self.orders[part]
                held = [0]
                for bit in bits[:step]:
                    held += [k + bit for k in held]
                for k in held:
                    self.items.append((part, step, k))
                    self.source[part, k + bits[step]] = (part, step, k)

    def copy(self, part, step, k):
        bit = self.orders[part][step]
        rows = pl.ds(part * self.half, self.half)
        source = self.own.at[rows, :] if k == 0 else self.slots.at[k, rows, :]
        return send(source, self.slots.at[k + bit, rows, :], self.sems, (part, step, k), other(self.me, bit, self.seq))

    def begin(self):
        for item in self.items:
            if item[2] == 0:
                self.copy(*item).start()

    def wait(self, part, k):
        if (part, k) not in self.arrived:
            self.arrived.add((part, k))
            self.copy(*self.source[part, k]).wait_recv()

    def forward(self):
        for item in self.items:
            if item[2] != 0:
                self.wait(item[0], item[2])
                self.copy(*item).start()

    def finish(self, k):
        self.wait(0, k)
        self.wait(1, k)

    def drain(self):
        for item in self.items:
            self.copy(*item).wait_send()

    @staticmethod
    def semaphores(seq):
        return pltpu.SemaphoreType.DMA((2, max(seq.bit_length() - 1, 1), seq))


class Spread:
    def __init__(self, here, dp, own, slots, sems):
        self.here, self.dp, self.own, self.slots = here, dp, own, slots
        self.far, self.near = sems[:2], sems[2:]

    def to_far(self, t):
        return send(self.own, self.slots.at[self.here], self.far, t, other(self.here, 2 * t, self.dp), "dp")

    def to_near(self, t):
        owner = other(self.here, 2 * t, self.dp)
        source = self.own if t == 0 else self.slots.at[owner]
        return send(source, self.slots.at[owner], self.near, t, other(self.here, 1, self.dp), "dp")

    def begin(self):
        for t in range(1, self.dp // 2):
            self.to_far(t).start()
        self.to_near(0).start()

    def forward(self):
        for t in range(1, self.dp // 2):
            self.to_far(t).wait_recv()
            self.to_near(t).start()

    def finish(self):
        for t in range(self.dp // 2):
            self.to_near(t).wait_recv()

    def drain(self):
        for t in range(1, self.dp // 2):
            self.to_far(t).wait_send()
        for t in range(self.dp // 2):
            self.to_near(t).wait_send()

    @staticmethod
    def semaphores(dp):
        return [pltpu.SemaphoreType.DMA((dp // 2,))] * 4


def selected(piece, offset, size, owner, wide, period):
    group = offset // PAIR
    lane = lax.broadcasted_iota(jnp.int32, (PAIR, wide), 0) - offset % PAIR
    place = lax.broadcasted_iota(jnp.int32, (PAIR, wide), 1) % period
    hot = (place == lane + owner * size) & (lane >= 0) & (lane < size)
    return nn(piece[:, group * PAIR:(group + 1) * PAIR], hot.astype(BF16))


def project_kernel(seq, dp, sizes, x_ref, wq_hbm, wkv_hbm, gain_ref, seg_ref,
                   x_hbm, a_hbm, q_hbm, kv_hbm, cos_hbm, sin_hbm, w_ref, g_attn, g_ffn, g_q, g_kv, starts_ref,
                   x_all, a_s, q_s, kv_s, cos_s, sin_s, start_s, pack_s, packs,
                   x_send, x_recv, far_out, far_in, near_out, near_in, in_sems, out_sems, table_sems):
    me, here = lax.axis_index("seq"), lax.axis_index("dp")
    rows, width = x_ref.shape
    depth = wq_hbm.shape[0]
    mine = q_s.shape[2]
    gather = Gather(me, seq, x_ref, x_all, (x_send, x_recv))
    pack = Spread(here, dp, pack_s, packs, (far_out, far_in, near_out, near_in))
    columns = pl.ds(pl.multiple_of(me * mine, mine), mine)
    loads = [pltpu.make_async_copy(wq_hbm.at[:, columns], pack_s.at[:depth, :mine], in_sems.at[0]),
             pltpu.make_async_copy(wkv_hbm.at[:, columns], pack_s.at[:depth, mine:], in_sems.at[1]),
             pltpu.make_async_copy(gain_ref, pack_s.at[depth:, :], in_sems.at[2])]
    for load in loads:
        load.start()

    def chunk(k):
        return pl.ds(pl.multiple_of(other(me, k, seq) * rows, rows), rows)

    def stores(k):
        return [pltpu.make_async_copy(x_ref if k == 0 else x_all.at[k], x_hbm.at[k], out_sems.at[0, k]),
                pltpu.make_async_copy(a_s.at[k], a_hbm.at[k], out_sems.at[1, k]),
                pltpu.make_async_copy(q_s.at[k], q_hbm.at[chunk(k), :], out_sems.at[2, k]),
                pltpu.make_async_copy(kv_s.at[k], kv_hbm.at[chunk(k), :], out_sems.at[3, k])]

    greet(seq, me, dp, here)
    gather.begin()
    for load in loads:
        load.wait()
    pack.begin()
    own = pltpu.make_async_copy(pack_s, packs.at[here], in_sems.at[3])
    own.start()

    seg = seg_ref[...]
    starts = jnp.zeros(seg.shape, F32)
    for doc in range(1, MOST_DOCS):
        begin = jnp.sum(jnp.where(seg < doc, 1.0, 0.0))
        starts = jnp.maximum(starts, jnp.where(seg >= doc, begin, 0.0))
    start_s[...] = starts
    starts_ref[...] = starts.astype(jnp.int32)
    lane = lanes((1, PAIR))
    frequency = jnp.exp((lane % (HEAD // 2)).astype(F32) * (-2.0 * math.log(THETA) / HEAD))
    sign = jnp.where(lane % HEAD < HEAD // 2, -1.0, 1.0)

    def table(p, _):
        at = pl.ds(pl.multiple_of(p * BLOCK, BLOCK), BLOCK)
        start = jnp.transpose(jnp.broadcast_to(start_s[pl.ds(p, 1), :], (BLOCK, BLOCK)))
        place = (p * BLOCK + lax.broadcasted_iota(jnp.int32, (BLOCK, PAIR), 0)).astype(F32)
        turned = (place - start) * frequency
        cos_s[at, :] = jnp.cos(turned)
        sin_s[at, :] = jnp.sin(turned) * sign
        return 0

    lax.fori_loop(0, seg.shape[0], table, 0)
    tables = [pltpu.make_async_copy(cos_s, cos_hbm, table_sems.at[0]),
              pltpu.make_async_copy(sin_s, sin_hbm, table_sems.at[1])]
    for copy in tables:
        copy.start()
    pack.forward()
    gather.forward()
    pack.finish()
    own.wait()
    totals = [jnp.zeros((16, width), F32)] * 2 + [jnp.zeros((16, mine), F32)] * 2
    for d in range(dp):
        w_ref[d * depth:(d + 1) * depth, :] = packs[d, :depth, :]
        piece = packs[d, depth:, :]
        for i, period in enumerate((width, width, HEAD, PAIR)):
            totals[i] = totals[i] + selected(piece, sum(sizes[:i]), sizes[i], d, totals[i].shape[1], period)
    gain = totals[0][0:1]
    g_attn[...] = totals[0][:8]
    g_ffn[...] = totals[1][:8]
    g_q[...] = totals[2][:8]
    g_kv[...] = jnp.where(lanes((8, mine)) % PAIR < HEAD, totals[3][:8], 1.0)
    for k in range(seq):
        if k:
            gather.finish(k)
        x = (x_ref[...] if k == 0 else x_all[k]).astype(F32)
        a = (x * lax.rsqrt(jnp.mean(x * x, axis=-1, keepdims=True) + EPS) * gain).astype(BF16)
        a_s[k] = a
        qkv = nn(a, w_ref[...])
        q_s[k] = qkv[:, :mine]
        kv_s[k] = qkv[:, mine:]
        for copy in stores(k):
            copy.start()
    gather.drain()
    pack.drain()
    for copy in tables:
        copy.wait()
    for k in range(seq):
        for copy in stores(k):
            copy.wait()


def project(x, w_query, w_keyval, gain_rows, segments, seq, dp, sizes):
    rows, width = x.shape
    wide = gain_rows.shape[1]
    mine = wide // 2
    depth = w_query.shape[0]
    whole, far = pl.BlockSpec(memory_space=VMEM), pl.BlockSpec(memory_space=pl.ANY)
    shape = jax.ShapeDtypeStruct
    dma = pltpu.SemaphoreType.DMA
    total = seq * rows
    return pl.pallas_call(
        functools.partial(project_kernel, seq, dp, sizes),
        out_shape=(
            shape((seq, rows, width), BF16), shape((seq, rows, width), BF16),
            shape((total, mine), F32), shape((total, mine), F32),
            shape((total, PAIR), F32), shape((total, PAIR), F32), shape((width, wide), BF16),
            shape((8, width), F32), shape((8, width), F32), shape((8, mine), F32), shape((8, mine), F32),
            shape(segments.shape, jnp.int32)),
        in_specs=[whole, far, far, whole, whole],
        out_specs=(far,) * 6 + (whole,) * 6,
        scratch_shapes=[
            VMEM((seq, rows, width), BF16), VMEM((seq, rows, width), BF16),
            VMEM((seq, rows, mine), F32), VMEM((seq, rows, mine), F32),
            VMEM((total, PAIR), F32), VMEM((total, PAIR), F32), VMEM(segments.shape, F32),
            VMEM((depth + 16, wide), BF16), VMEM((dp, depth + 16, wide), BF16),
            Gather.semaphores(seq), Gather.semaphores(seq)]
        + Spread.semaphores(dp) + [dma((4,)), dma((4, seq)), dma((2,))],
        compiler_params=pltpu.CompilerParams(vmem_limit_bytes=LIMIT, collective_id=0, has_side_effects=True),
        name="project",
    )(x, w_query, w_keyval, gain_rows, segments)


def ffn_kernel(seq, *refs):
    refs = list(refs)
    o_ref, x_hbm, gain, w_hbm = refs[:4]
    gy_hbm = refs[4:4 + seq]
    rest = refs[4 + seq:]
    grad_hbm, dx_ref, xy_ref, do_ref = rest[:4]
    y_hbm = [None] + rest[4:3 + seq]
    (w, w_out, total, o_buf, x_s, gy_s, x1_s, db_s, db_t, y_out, db_send, db_recv, held, extra,
     w_sems, o_send, o_recv, db_out, db_in, do_out, do_in, in_sems, y_sem, extra_sem) = rest[3 + seq:]
    me = lax.axis_index("seq")
    pieces, _, width = w_hbm.shape
    depth = width // pieces
    part = (w_hbm.shape[1] - depth) // 3
    rows = dx_ref.shape[0]
    half = rows // 2
    cols = o_ref.shape[1]
    relay = seq == 4

    def load_w(k, d):
        source = w_hbm.at[d, pl.ds(k * part, depth if k == 3 else part), :]
        target = w_out.at[pl.ds(d * depth, depth), :] if k == 3 else w.at[k, pl.ds(d * part, part), :]
        return pltpu.make_async_copy(source, target, w_sems.at[k, d])

    def store_w(k, d):
        source = w_out.at[pl.ds(d * depth, depth), :] if k == 3 else w.at[k, pl.ds(d * part, part), :]
        return pltpu.make_async_copy(
            source, grad_hbm.at[d, pl.ds(k * part, depth if k == 3 else part), :], w_sems.at[k, d])

    def store_extra(d):
        return pltpu.make_async_copy(extra, grad_hbm.at[d, pl.ds(3 * part + depth, 16), :], extra_sem.at[d])

    def rows_of(device, h):
        return pl.ds(pl.multiple_of(device * rows + h * half, half), half)

    def half_at(h):
        return pl.ds(pl.multiple_of(h * half, half), half)

    def load_x(k, h):
        return pltpu.make_async_copy(x_hbm.at[k, half_at(h), :], x_s.at[h], in_sems.at[0, h])

    def load_gy(k, h):
        return pltpu.make_async_copy(gy_hbm[k].at[half_at(h), :], gy_s.at[h], in_sems.at[1, h])

    def start_inputs(k, h):
        load_x(k, h).start()
        for one in range(seq):
            @pl.when(k == one)
            def _():
                load_gy(one, h).start()

    def store_y(k, h):
        return pltpu.make_async_copy(y_out, y_hbm[k].at[half_at(h), :], y_sem)

    def send_o(k, h, j):
        peer = other(me, j, seq)
        return send(o_ref.at[rows_of(other(peer, k, seq), h), :], o_buf.at[k, h, j - 1],
                    (o_send, o_recv), (k, h, j - 1), peer)

    def pass_o(k, h, j, target, peer):
        return send(o_buf.at[k, h, j - 1], o_buf.at[target, h, 2], (o_send, o_recv), (target, h, 2),
                    other(me, peer, seq))

    def starts_o(k):
        for h in range(2):
            for j in reversed(range(1, seq)):
                if not relay or j < 3:
                    send_o(k, h, j).start()
                elif not isinstance(k, int):
                    pass
                elif k == 3:
                    send_o(k, h, j).start()

    def send_db(k, h, peer):
        return send(db_send.at[k - 1, half_at(h), :], db_recv.at[k - 1, half_at(h), :], (db_out, db_in), (k - 1, h),
                    other(me, peer, seq))

    def out_rows(j):
        return pl.ds(pl.multiple_of(other(me, j, seq) * cols, cols), cols)

    for k in (3, 0, 1, 2):
        for d in range(pieces):
            load_w(k, d).start()
    start_inputs(seq - 1, 0)
    greet(seq, me)
    starts_o(seq - 1)
    if seq > 1:
        starts_o(seq - 2)
    total[...] = jnp.zeros_like(total)
    for k in range(4):
        for d in range(pieces):
            load_w(k, d).wait()

    def one_part(i, _):
        k = seq - 1 - i // 2
        h = i % 2
        load_x(0, h).wait()
        load_gy(0, h).wait()

        @pl.when(i < 2 * seq - 1)
        def _():
            start_inputs(seq - 1 - (i + 1) // 2, 1 - h)

        for j in range(1, seq):
            send_o(k, h, j).wait_recv()
        if relay:
            @pl.when(k == 3)
            def _():
                pass_o(3, h, 2, 2, 1).start()
                pass_o(3, h, 1, 1, 2).start()

            @pl.when((k == 2) & (h == 0))
            def _():
                pass_o(2, 0, 1, 0, 2).start()

            @pl.when((k == 1) & (h == 1))
            def _():
                pass_o(1, 1, 2, 0, 1).start()

        x1 = x_s[h].astype(F32) + nn(o_ref[rows_of(other(me, k, seq), h), :], w_out[out_rows(0), :])
        for j in range(1, seq):
            x1 = x1 + nn(o_buf[k, h, j - 1], w_out[out_rows(j), :])
        x1_s[half_at(h), :] = x1
        scale = lax.rsqrt(jnp.mean(x1 * x1, axis=-1, keepdims=True) + EPS)
        b = (x1 * scale * gain[0:1, :]).astype(BF16)
        gy = gy_s[h]
        gate = nt(b, w[0])
        up = nt(b, w[1])
        d_act = nt(gy, w[2])
        sig = jax.nn.sigmoid(gate)
        silu = gate * sig
        act = (silu * up).astype(BF16)
        d_gate = (d_act * up * sig * (1.0 + gate * (1.0 - sig))).astype(BF16)
        d_up = (d_act * silu).astype(BF16)
        total[0] += tn(d_gate, b)
        total[1] += tn(d_up, b)
        total[2] += tn(act, gy)
        db_t[...] = nn(d_gate, w[0]) + nn(d_up, w[1])
        y = nn(act, w[2])

        @pl.when(k == 0)
        def _():
            xy_ref[half_at(h), :] = x1_s[half_at(h), :] + y
            db_s[half_at(h), :] = db_t[...]

        if relay:
            for one, when, near in ((2, 0, 1), (1, 1, 2)):
                @pl.when((k == one) & (h == when))
                def _():
                    send_db(3, when, near).wait_recv()
                    db_t[...] += db_recv[2, when * half:(when + 1) * half, :].astype(F32)

        @pl.when(k > 0)
        def _():
            @pl.when(i > 0)
            def _():
                store_y(1, 0).wait()

            y_out[...] = y.astype(BF16)
            db_send[k - 1, half_at(h), :] = db_t[...].astype(BF16)
            for one in range(1, seq):
                @pl.when(k == one)
                def _():
                    store_y(one, h).start()
                    if not relay or one < 3:
                        send_db(one, h, one).start()
            if relay:
                @pl.when(i == 0)
                def _():
                    send_db(3, 0, 1).start()

                @pl.when(i == 1)
                def _():
                    send_db(3, 1, 2).start()

        for one in range(2, seq):
            @pl.when((k == one) & (h == 1))
            def _():
                starts_o(one - 2)

        return 0

    lax.fori_loop(0, 2 * seq, one_part, 0)
    db = db_s[...]
    for k in reversed(range(1, 3 if relay else seq)):
        for h in range(2):
            send_db(k, h, k).wait_recv()
        db = db + db_recv[k - 1].astype(F32)
    x1 = x1_s[...]
    factor = lax.rsqrt(jnp.mean(x1 * x1, axis=-1, keepdims=True) + EPS)
    unit = x1 * factor
    term = db * unit
    weighted = db * gain[0:1, :]
    back = factor * (weighted - unit * jnp.mean(term * gain[0:1, :], axis=-1, keepdims=True))
    dx = jnp.concatenate([gy_s[0], gy_s[1]], axis=0).astype(F32) + back
    dx_ref[...] = dx
    dy = dx.astype(BF16)

    def send_do(j):
        mine = pl.ds(pl.multiple_of(me * rows, rows), rows)
        return send(held.at[j - 1], do_ref.at[mine, :], (do_out, do_in), j - 1, other(me, j, seq))

    for j in reversed(range(1, seq)):
        held[j - 1] = nt(dy, w_out[out_rows(j), :]).astype(BF16)
        send_do(j).start()
    do_ref[pl.ds(pl.multiple_of(me * rows, rows), rows), :] = nt(dy, w_out[out_rows(0), :]).astype(BF16)
    extra[...] = jnp.broadcast_to(jnp.sum(term, axis=0, keepdims=True), (16, width)).astype(BF16)
    for j in range(seq):
        grad = 0.0
        for h in range(2):
            o = o_ref[rows_of(me, h), :] if j == 0 else o_buf[0, h, j - 1]
            grad = grad + tn(o, dy[h * half:(h + 1) * half])
        w_out[out_rows(j), :] = grad.astype(BF16)
    for d in range(pieces):
        store_extra(d).start()
        store_w(3, d).start()
    for k in range(3):
        w[k] = total[k].astype(BF16)
        for d in range(pieces):
            store_w(k, d).start()
    for j in range(1, seq):
        send_do(j).wait_send()
        send_do(j).wait_recv()
        for k in range(seq):
            for h in range(2):
                send_o(k, h, j).wait_send()
    for k in range(1, seq):
        for h in range(2):
            send_db(k, h, k).wait_send()
    store_y(1, 0).wait()
    for d in range(pieces):
        store_extra(d).wait()
        for k in range(4):
            store_w(k, d).wait()


def ffn(o, x, gy, gain, w):
    seq = len(gy)
    all_rows, cols = o.shape
    rows, width = gy[0].shape
    pieces = w.shape[0]
    depth = width // pieces
    part = (w.shape[1] - depth) // 3
    hidden = pieces * part
    half = rows // 2
    whole, far = pl.BlockSpec(memory_space=VMEM), pl.BlockSpec(memory_space=pl.ANY)
    shape = jax.ShapeDtypeStruct
    dma = pltpu.SemaphoreType.DMA
    return pl.pallas_call(
        functools.partial(ffn_kernel, seq),
        out_shape=(shape((pieces, 3 * part + depth + 16, width), BF16), shape((rows, width), F32),
                   shape((rows, width), F32), shape((all_rows, cols), BF16))
        + (shape((rows, width), BF16),) * (seq - 1),
        in_specs=[whole, far, whole, far] + [far] * seq,
        out_specs=(far,) + (whole,) * 3 + (far,) * (seq - 1),
        scratch_shapes=[
            VMEM((3, hidden, width), BF16),
            VMEM((width, width), BF16),
            VMEM((3, hidden, width), F32),
            VMEM((seq, 2, seq - 1, half, cols), BF16),
            VMEM((2, half, width), BF16),
            VMEM((2, half, width), BF16),
            VMEM((rows, width), F32),
            VMEM((rows, width), F32),
            VMEM((half, width), F32),
            VMEM((half, width), BF16),
            VMEM((seq - 1, rows, width), BF16),
            VMEM((seq - 1, rows, width), BF16),
            VMEM((seq - 1, rows, cols), BF16),
            VMEM((16, width), BF16),
            dma((4, pieces)), dma((seq, 2, seq - 1)), dma((seq, 2, seq - 1)), dma((seq - 1, 2)), dma((seq - 1, 2)),
            dma((seq - 1,)), dma((seq - 1,)), dma((2, 2)), dma(()), dma((pieces,)),
        ],
        compiler_params=pltpu.CompilerParams(vmem_limit_bytes=LIMIT, collective_id=1, has_side_effects=True),
        name="ffn",
    )(o, x, gain, w, *gy)


class Reduce:
    def __init__(self, here, dp, pieces, near, out, far, sems):
        self.here, self.dp, self.pieces, self.near, self.out, self.far = here, dp, pieces, near, out, far
        self.sems = sems

    def to_near(self, t):
        mate = other(self.here, 1, self.dp)
        return send(self.pieces.at[other(mate, 2 * t, self.dp)], self.near.at[t], self.sems[2:], t, mate, "dp")

    def to_far(self, t):
        return send(self.out.at[t - 1], self.far.at[t - 1], self.sems[:2], t, other(self.here, 2 * t, self.dp), "dp")

    def begin(self):
        for t in reversed(range(self.dp // 2)):
            self.to_near(t).start()

    def pair(self, t):
        return self.pieces[other(self.here, 2 * t, self.dp)].astype(F32) + self.near[t].astype(F32)

    def middle(self):
        for t in reversed(range(1, self.dp // 2)):
            self.to_near(t).wait_recv()
            self.out[t - 1] = self.pair(t).astype(BF16)
            self.to_far(t).start()

    def finish(self):
        self.to_near(0).wait_recv()
        total = self.pair(0)
        for t in range(1, self.dp // 2):
            self.to_far(t).wait_recv()
            total = total + self.far[t - 1].astype(F32)
        return total

    def drain(self):
        for t in range(self.dp // 2):
            self.to_near(t).wait_send()
        for t in range(1, self.dp // 2):
            self.to_far(t).wait_send()

    @staticmethod
    def scratch(dp, rows, wide):
        return [VMEM((dp // 2, rows, wide), BF16)] + [VMEM((dp // 2 - 1, rows, wide), BF16)] * 2

    @staticmethod
    def semaphores(dp):
        return [pltpu.SemaphoreType.DMA((dp // 2,))] * 4


def project_back_kernel(seq, dp, *refs):
    refs = list(refs)
    dq, dkv, gains, w, g_attn, a_hbm, x_hbm, dx_hbm, xy_hbm = refs[:9]
    y_hbm = refs[9:8 + seq]
    (grad_x, out_ref, gwq_ref, gwkv_ref, gain_out, a_all, x_s, dx_s, xy_s, y_s, acc, da, arrived, pieces, results,
     q_near, q_out, q_far, rs_out, rs_in, q1, q2, q3, q4, all_out, all_in, in_sems) = refs[8 + seq:]
    me, here = lax.axis_index("seq"), lax.axis_index("dp")
    rows, width = x_s.shape
    mine = dq.shape[1]
    depth = width // dp
    half = rows // 2
    orders = flips(seq)
    red_q = Reduce(here, dp, pieces, q_near, q_out, q_far, (q1, q2, q3, q4))
    loads = [pltpu.make_async_copy(a_hbm, a_all, in_sems.at[0]), pltpu.make_async_copy(xy_hbm, xy_s, in_sems.at[1])]
    loads += [pltpu.make_async_copy(y_hbm[k], y_s.at[k], in_sems.at[2 + k]) for k in range(seq - 1)]
    loads += [pltpu.make_async_copy(x_hbm, x_s, in_sems.at[1 + seq]),
              pltpu.make_async_copy(dx_hbm, dx_s, in_sems.at[2 + seq])]
    for load in loads:
        load.start()

    def chunk(k):
        return pl.ds(pl.multiple_of(other(me, k, seq) * rows, rows), rows)

    def pass_on(part, step, k):
        return send(acc.at[k, pl.ds(part * half, half), :], arrived.at[part, k - 1], (rs_out, rs_in),
                    (part, step, k), other(me, orders[part][step], seq))

    def sent_at(part, step):
        before = sum(orders[part][:step])
        return [k for k in range(1, seq) if k & orders[part][step] and not k & before]

    def to_all(j):
        return send(results.at[me], results.at[me], (all_out, all_in), j - 1, other(me, j, seq))

    def partial_da(k):
        return nt(dq[chunk(k), :], w[:, :mine]) + nt(dkv[chunk(k), :], w[:, mine:])

    greet(seq, me, dp, here)
    for k in reversed(range(1, seq)):
        acc[k] = partial_da(k).astype(BF16)
        for part in range(2):
            if k in sent_at(part, 0):
                pass_on(part, 0, k).start()
    loads[0].wait()
    for d in range(2):
        grads = dq if d == 0 else dkv
        total = tn(a_all[0], grads[chunk(0), :])
        for k in range(1, seq):
            total = total + tn(a_all[k], grads[chunk(k), :])
        pieces[:, :depth, d * mine:(d + 1) * mine] = total.astype(BF16).reshape(dp, depth, mine)
        sum8 = jnp.sum(gains[8 * d:8 * d + 8, :], axis=0, keepdims=True)
        pieces[:, depth:, d * mine:(d + 1) * mine] = jnp.broadcast_to(sum8[None], (dp, 16, mine)).astype(BF16)
    red_q.begin()
    da[...] = partial_da(0)
    red_q.middle()
    for load in loads[1:]:
        load.wait()
    out = xy_s[...]
    for k in range(seq - 1):
        out = out + y_s[k].astype(F32)
    out_ref[...] = out.astype(BF16)
    for step in range(len(orders[0])):
        for part in range(2):
            at = pl.ds(part * half, half)
            for k in sent_at(part, step):
                pass_on(part, step, k).wait_recv()
                target = k - orders[part][step]
                if target == 0:
                    da[at, :] += arrived[part, k - 1].astype(F32)
                else:
                    acc[target, at, :] = (acc[target, at, :].astype(F32) + arrived[part, k - 1].astype(F32)).astype(BF16)
            if step + 1 < len(orders[0]):
                for k in sent_at(part, step + 1):
                    pass_on(part, step + 1, k).start()
        if step == 0:
            results[me] = red_q.finish().astype(BF16)
            for j in reversed(range(1, seq)):
                to_all(j).start()
    x = x_s[...].astype(F32)
    factor = lax.rsqrt(jnp.mean(x * x, axis=-1, keepdims=True) + EPS)
    unit = x * factor
    weighted = da[...] * g_attn[0:1, :]
    grad_x[...] = dx_s[...] + factor * (weighted - unit * jnp.mean(weighted * unit, axis=-1, keepdims=True))
    for j in range(1, seq):
        to_all(j).wait_recv()
    gain_total = jnp.zeros((16, 2 * mine), F32)
    for j in range(seq):
        gwq_ref[:, j * mine:(j + 1) * mine] = results[j, :depth, :mine].astype(F32)
        gwkv_ref[:, j * mine:(j + 1) * mine] = results[j, :depth, mine:].astype(F32)
        gain_total = gain_total + results[j, depth:, :].astype(F32)
    gain_out[...] = gain_total
    for j in range(1, seq):
        to_all(j).wait_send()
    for part in range(2):
        for step in range(len(orders[0])):
            for k in sent_at(part, step):
                pass_on(part, step, k).wait_send()
    red_q.drain()


def project_back(dq, dkv, gains, a_all, w_qkv, dp, x, dx, g_attn, xy, y_parts):
    seq, rows, width = a_all.shape
    depth = width // dp
    mine = dq.shape[1]
    whole, far = pl.BlockSpec(memory_space=VMEM), pl.BlockSpec(memory_space=pl.ANY)
    shape = jax.ShapeDtypeStruct
    dma = pltpu.SemaphoreType.DMA
    steps = seq.bit_length() - 1
    return pl.pallas_call(
        functools.partial(project_back_kernel, seq, dp),
        out_shape=(shape((rows, width), F32), shape((rows, width), BF16), shape((depth, seq * mine), F32),
                   shape((depth, seq * mine), F32), shape((16, 2 * mine), F32)),
        in_specs=[whole] * 5 + [far] * (3 + seq),
        out_specs=(whole,) * 5,
        scratch_shapes=[
            VMEM((seq, rows, width), BF16),
            VMEM((rows, width), BF16),
            VMEM((rows, width), F32),
            VMEM((rows, width), F32),
            VMEM((seq - 1, rows, width), BF16),
            VMEM((seq, rows, width), BF16),
            VMEM((rows, width), F32),
            VMEM((2, seq - 1, rows // 2, width), BF16),
            VMEM((dp, depth + 16, 2 * mine), BF16),
            VMEM((seq, depth + 16, 2 * mine), BF16),
            *Reduce.scratch(dp, depth + 16, 2 * mine),
            dma((2, steps, seq)), dma((2, steps, seq)),
            *Reduce.semaphores(dp), dma((seq - 1,)), dma((seq - 1,)), dma((3 + seq,)),
        ],
        compiler_params=pltpu.CompilerParams(vmem_limit_bytes=LIMIT, collective_id=3, has_side_effects=True),
        name="project_back",
    )(dq, dkv, gains, w_qkv, g_attn, a_all, x, dx, xy, *y_parts)


def share_kernel(seq, own, grads_ref, out_ref, extra_ref, slots, send_sem, recv_sem):
    me = lax.axis_index("seq")
    gather = Gather(me, seq, own, slots, (send_sem, recv_sem))
    part = grads_ref.shape[2]
    depth = out_ref.shape[0]
    greet(seq, me)
    gather.begin()
    out_ref[...] = own[3 * part:3 * part + depth, :].astype(F32)
    extra_ref[...] = own[3 * part + depth:, :].astype(F32)
    for k in range(3):
        grads_ref[k, me] = own[k * part:(k + 1) * part, :].astype(F32)
    gather.forward()
    for j in range(1, seq):
        gather.finish(j)
        for k in range(3):
            grads_ref[k, other(me, j, seq)] = slots[j, k * part:(k + 1) * part, :].astype(F32)
        out_ref[...] += slots[j, 3 * part:3 * part + depth, :].astype(F32)
        extra_ref[...] += slots[j, 3 * part + depth:, :].astype(F32)
    gather.drain()


def share(own, seq, part, depth):
    rows, width = own.shape
    whole = pl.BlockSpec(memory_space=VMEM)
    shape = jax.ShapeDtypeStruct
    return pl.pallas_call(
        functools.partial(share_kernel, seq),
        out_shape=(shape((3, seq, part, width), F32), shape((depth, width), F32),
                   shape((rows - 3 * part - depth, width), F32)),
        in_specs=[whole],
        out_specs=(whole,) * 3,
        scratch_shapes=[VMEM((seq, rows, width), BF16), Gather.semaphores(seq), Gather.semaphores(seq)],
        compiler_params=pltpu.CompilerParams(vmem_limit_bytes=LIMIT, collective_id=4, has_side_effects=True),
        name="share",
    )(own)


def exchanged(u, bits, seq):
    return lax.ppermute(u, "seq", [(i, i ^ bits) for i in range(seq)])


def packed_order(order_row, starts):
    blocks = order_row.shape[0]
    ids = jnp.arange(blocks, dtype=jnp.int32)
    inv = jnp.sum(jnp.where(order_row[None, :] == ids[:, None], ids[None, :], 0), axis=1, dtype=jnp.int32)
    return inv, starts[:, 0] // BLOCK


def shards(tokens_in, norm_attn, w_query, w_keyval, gain_query, gain_key, w_out, norm_ffn,
           w_gate, w_up, w_down, cotangent, segments, blocks):
    seq, dp = lax.axis_size("seq"), lax.axis_size("dp")
    me = lax.axis_index("seq")
    rows, width = tokens_in.shape
    total_rows = rows * seq
    mine = KEY_VALUE_HEADS // seq * PAIR
    depth = w_query.shape[0]
    part = w_down.shape[0] // seq

    gain_row = jnp.concatenate([norm_attn, norm_ffn, gain_query, gain_key])
    sizes = (norm_attn.shape[0], norm_ffn.shape[0], gain_query.shape[0], gain_key.shape[0])
    gain_rows = jnp.pad(gain_row[None, :], ((0, 15), (0, 2 * mine - gain_row.shape[0])))
    def my_rows(u):
        return lax.dynamic_slice_in_dim(u, me * part, part, 0)

    ffn_w = jnp.concatenate([my_rows(w_gate.T), my_rows(w_up.T), my_rows(w_down), w_out])
    ffn_w = lax.all_gather(ffn_w, "dp", axis=0)
    in_pieces = part % 16 == 0
    if not in_pieces:
        body = jnp.moveaxis(ffn_w[:, :3 * part].reshape(dp, 3, part, width), 0, 1)
        ffn_w = jnp.concatenate([body.reshape(-1, width), ffn_w[:, 3 * part:].reshape(-1, width)])[None]

    (x_all, a_all, q_raw, kv_raw, cos, sin, w_qkv, g_attn, g_ffn, gain_q, gain_kv, starts) = project(
        tokens_in, w_query, w_keyval, gain_rows, segments.reshape(-1, BLOCK), seq, dp, sizes)
    inv, first = packed_order(blocks[0], starts)
    gy, q_raw = lax.optimization_barrier((cotangent, q_raw))
    gy_all = [gy] + [exchanged(gy, k, seq) for k in range(1, seq)]
    o, qs, kvs, linv = attend(inv, first, q_raw, kv_raw, cos, sin, starts, gain_q, gain_kv)

    ffn_grads, d_x1, x1_y, d_o, *y_parts = ffn(o, x_all, gy_all, g_ffn, ffn_w)
    if not in_pieces:
        body = jnp.moveaxis(ffn_grads[0, :3 * dp * part].reshape(3, dp, part, width), 1, 0)
        out = ffn_grads[0, 3 * dp * part:-16].reshape(dp, depth, width)
        extra = jnp.broadcast_to(ffn_grads[0, None, -16:], (dp, 16, width))
        ffn_grads = jnp.concatenate([body.reshape(dp, 3 * part, width), out, extra], 1)
        ffn_grads = jnp.pad(ffn_grads, ((0, 0), (0, -ffn_grads.shape[1] % 32), (0, 0)))
    ffn_grads = lax.psum_scatter(ffn_grads, "dp", scatter_dimension=0, tiled=True)[0]

    y_parts = [exchanged(y_parts[k - 1], k, seq) for k in range(1, seq)]
    dq_raw, dkv_raw, gain_sums = attend_back(
        inv, first, q_raw, kv_raw, cos, sin, starts, gain_q, gain_kv, o, d_o, qs, kvs, linv)
    grad_tokens, output, grad_wq, grad_wkv, gain_sums = project_back(
        dq_raw, dkv_raw, gain_sums, a_all, w_qkv, dp, tokens_in, d_x1, g_attn, x1_y, y_parts)
    ffn_grads, grad_wout, extra = share(ffn_grads, seq, part, depth)
    ffn_grads = ffn_grads.reshape(3, seq * part, width)

    here = lax.axis_index("dp")

    def owned(vector, size):
        return lax.dynamic_slice_in_dim(vector, here * size, size)

    d_g_ffn = owned(extra[0], sizes[1])
    d_g_query = owned(jnp.sum(gain_sums[0, :mine].reshape(-1, HEAD), 0), sizes[2])
    d_g_key = owned(jnp.sum(gain_sums[0, mine:].reshape(-1, PAIR)[:, :HEAD], 0), sizes[3])
    d_g_attn = jnp.sum(grad_wq * w_query.astype(F32) + grad_wkv * w_keyval.astype(F32), axis=1)
    d_g_attn = d_g_attn / norm_attn.astype(F32)
    return (output, grad_tokens, d_g_attn, grad_wq, grad_wkv, d_g_query, d_g_key, grad_wout, d_g_ffn,
            ffn_grads[0].T, ffn_grads[1].T, ffn_grads[2])


def solution(mesh):
    rows, cols, row2 = P("dp", None), P(None, "dp"), P(("dp", "seq"), None)
    vec = P("dp")
    return jax.shard_map(
        shards,
        mesh=mesh,
        in_specs=(row2, vec, rows, rows, vec, vec, rows, vec, cols, cols, rows, row2, rows, rows),
        out_specs=(row2, row2, vec, rows, rows, vec, vec, rows, vec, cols, cols, rows),
        check_vma=False,
    )
```
